512 devices in a mesh: tm: 256 (over z, y, x), state: 2 (over core).
Axes of the slice: x: 4, y: 8, z: 8, core: 2. Of those that a mesh axis runs over, the one named last changes fastest.
Arguments:
- features: float32 [4, 4096, 512], P(None, 'tm'), may hold values from -18 to 18
- gauss_means: float32 [1024, 512], P('state'), may hold values from -3 to 3
- precisions: float32 [1024, 512], P('state'), may hold values from 0.5 to 2
- transitions: bfloat16 [1024, 1024], P('state'), may hold values from 0 to 1, as said below
- initial: bfloat16 [1024], P('state'), may hold values from 0.099609375 to 10
- reset_flags: int32 [4, 4096], P(None, 'tm'), may hold values from 0 to 1, as said below
Outputs:
- posteriors: bfloat16 [4, 4096, 1024], P(None, 'tm', 'state')
- evidence: float32 [4, 4096], P(None, ('tm', 'state'))
The draws below stay inside these ranges and needn't reach their ends.
Inputs may be any that keep to these rules, and one draw needn't show every extreme that they name: `transitions`: every entry nonnegative; each row sums to 1 up to the rounding of its entries; the diagonal holds half or more of each row. reset_flags[b, 0] = 1 in every stream; the runs of frames from one 1 to the next (utterances) hold 1 to 16 frames, and some hold exactly 16.
All inputs are finite; a program needn't handle non-finite values.
Results may differ from the reference program's by a relative error of at most 0.012.
Values may be sent and summed in bfloat16 or wider, within the bound.
No kernel may reach another device: no remote copies, remote signals or barrier semaphores. Data moves between devices by JAX's collectives and lax.ppermute only.
A program may use at most 64 MiB of HBM per device.

```python
import math
import jax
import jax.numpy as jnp
from jax import lax

S = 1024
F = 512
STREAMS = 4
MAXLEN = 16
FRAMES = 4096


def draw_features(key, part):
    noise = jnp.clip(jax.random.normal(jax.random.fold_in(key, 11), (STREAMS, FRAMES, F), jnp.float32), -6.0, 6.0)
    frame_scale = jnp.exp(jax.random.uniform(jax.random.fold_in(key, 12), (STREAMS, FRAMES, 1), jnp.float32, jnp.log(0.5), jnp.log(3.0)))
    return noise * frame_scale


def draw_transitions(key, part):
    staying = jax.random.uniform(jax.random.fold_in(key, 21), (S,), jnp.float32, 0.5, 0.9)
    leaving = jnp.exp(jax.random.uniform(jax.random.fold_in(key, 22), (S, S), jnp.float32, jnp.log(0.1), jnp.log(10.0)))
    leaving = leaving * (1.0 - jnp.eye(S, dtype=jnp.float32))
    leaving = leaving / jnp.sum(leaving, axis=1, keepdims=True) * (1.0 - staying)[:, None]
    return (leaving + jnp.diag(staying)).astype(jnp.bfloat16)


def draw_reset_flags(key, part):
    shortest = max(MAXLEN // 2, 1)
    count = FRAMES // shortest + 2
    lengths = jax.random.randint(jax.random.fold_in(key, 31), (STREAMS, count), shortest, MAXLEN + 1)
    lengths = lengths.at[:, 0].set(MAXLEN - 1)
    lengths = lengths.at[:, 1].set(MAXLEN)
    starts = jnp.cumsum(lengths, axis=1) - lengths

    def marked(row_starts):
        return jnp.zeros((FRAMES,), jnp.int32).at[row_starts].set(1, mode='drop')
    return jax.vmap(marked)(starts)


def block_scale(rng, shape, pieces, low, high):
    def one(axis_at, shards_of):
        draws = jax.random.uniform(jax.random.fold_in(jax.random.fold_in(rng, 6), axis_at), (shards_of,), jnp.float32, low / len(pieces), high / len(pieces))
        return jnp.repeat(jnp.exp(draws), shape[axis_at] // shards_of).reshape((-1,) + (1,) * (len(shape) - axis_at - 1))

    level = one(*pieces[0])
    for cut in pieces[1:]:
        level = level * one(*cut)
    return level


def scatter_about(rng, dims, scale, reach, cuts=(), kind=jnp.bfloat16):
    gain = block_scale(rng, dims, cuts, -0.22, 0.18) if cuts else 1.0
    values = jax.random.normal(rng, dims, jnp.float32) * scale * gain
    return jnp.minimum(jnp.maximum(values, -reach), reach).astype(kind)


def setup_inputs(seed: int = 0) -> dict:
    streams_of = jax.random.split(jax.random.key(seed), 7)
    features = draw_features(jax.random.fold_in(streams_of[6], 71), 0)
    gauss_means = scatter_about(streams_of[1], (S, F), 0.5, 3.0, ((0, 2),), jnp.float32)
    precisions = jnp.clip(jnp.exp(math.log(2.0) - 1.3862944 * jax.random.uniform(streams_of[2], (S, F), jnp.float32) ** block_scale(streams_of[2], (S, F), ((0, 2),), -0.2, 0.2)), 0.5, 2.0)
    transitions = draw_transitions(jax.random.fold_in(streams_of[6], 71), 0)
    initial = jnp.clip(jnp.exp(math.log(10.0) - 4.609084 * jax.random.uniform(streams_of[4], (S,), jnp.float32) ** block_scale(streams_of[4], (S,), ((0, 2),), -0.2, 0.2)), 0.099609375, 10.0).astype(jnp.bfloat16)
    reset_flags = draw_reset_flags(jax.random.fold_in(streams_of[6], 71), 0)
    return dict(features=features, gauss_means=gauss_means, precisions=precisions, transitions=transitions, initial=initial, reset_flags=reset_flags)


acoustic = 0.1


def reference(features, gauss_means, precisions, transitions, initial, reset_flags):
    streams, frames, feat_width = features.shape
    states = gauss_means.shape[0]
    highest = lax.Precision.HIGHEST
    flat_feats = features.reshape(streams * frames, feat_width)
    quadratic = jnp.dot(flat_feats * flat_feats, (-0.5 * precisions).T, precision=highest)
    linear_part = jnp.dot(flat_feats, (precisions * gauss_means).T, precision=highest)
    offset = 0.5 * jnp.sum(jnp.log(precisions) - precisions * gauss_means * gauss_means, axis=1)
    scores = (acoustic * (quadratic + linear_part + offset)).reshape(streams, frames, states)
    maxima = jnp.max(scores, axis=2, keepdims=True)
    emission_t = jnp.swapaxes(jnp.exp(scores - maxima), 0, 1)
    reset_t = jnp.swapaxes(reset_flags, 0, 1)
    prior_float = initial.astype(jnp.float32)
    prior_dist = prior_float / jnp.sum(prior_float)
    trans_back = transitions.T

    def forward_step(alpha_prev, inputs):
        emit_row, reset_row = inputs
        predicted = jnp.dot(alpha_prev.astype(jnp.bfloat16), transitions, preferred_element_type=jnp.float32)
        predicted = jnp.where(reset_row[:, None] == 1, prior_dist[None, :], predicted)
        weighted = emit_row * predicted
        norm_total = jnp.sum(weighted, axis=1)
        alpha_next = weighted / norm_total[:, None]
        return alpha_next, (alpha_next, jnp.log(norm_total))

    alpha_start = jnp.zeros((streams, states), jnp.float32)
    alpha_last, (alphas, log_norms) = lax.scan(forward_step, alpha_start, (emission_t, reset_t))

    def backward_step(beta_next, inputs):
        emit_row, reset_row = inputs
        spread = jnp.dot((emit_row * beta_next).astype(jnp.bfloat16), trans_back, preferred_element_type=jnp.float32)
        spread = spread / jnp.sum(spread, axis=1, keepdims=True)
        beta_prev = jnp.where(reset_row[:, None] == 1, 1.0 / states, spread)
        return beta_prev, beta_next

    beta_start = jnp.full((streams, states), 1.0 / states, jnp.float32)
    beta_first, betas = lax.scan(backward_step, beta_start, (emission_t, reset_t), reverse=True)
    product = alphas * betas
    posterior = (product / jnp.sum(product, axis=2, keepdims=True)).astype(jnp.bfloat16)
    return jnp.swapaxes(posterior, 0, 1), jnp.swapaxes(log_norms, 0, 1)
```

```python
import jax
import jax.numpy as jnp
from jax import lax
from jax.experimental import pallas as pl
from jax.experimental.pallas import tpu as pltpu
from jax.sharding import PartitionSpec as P

MAXLEN = 16
acoustic = 0.1
VMEM = pltpu.VMEM


def split_pair(x):
    high = x.astype(jnp.bfloat16)
    return high, (x - high.astype(jnp.float32)).astype(jnp.bfloat16)


def prepare_kernel(feats, means, precs, trans, init, flags, send, keep_t, pack):
    core = lax.axis_index("state")
    half, width = means.shape
    rows = feats.shape[0]
    streams, frames = flags.shape
    init_row = init[...].astype(jnp.float32).reshape(1, half)
    for c in range(width // 128):
        at = slice(128 * c, 128 * c + 128)
        pack[c, 0:rows, :] = feats[:, at]
        pack[c, rows : rows + 8, :] = jnp.broadcast_to(init_row[:, at], (8, 128))
    flags_float = flags[...].astype(jnp.float32)
    pack[0, rows + 4 : rows + 4 + streams, 0:frames] = flags_float
    pack[0, rows + 4 : rows + 4 + streams, frames : 2 * frames] = flags_float

    prec = precs[...]
    mean = means[...]
    scaled = prec * mean
    quad_hi, quad_lo = split_pair((-0.5 * acoustic) * prec)
    lin_hi, lin_lo = split_pair(acoustic * scaled)
    send[0:half, 0:width] = quad_hi
    send[0:half, width : 2 * width] = lin_hi
    send[0:half, 2 * width : 3 * width] = quad_lo
    send[0:half, 3 * width : 4 * width] = lin_lo
    terms_hi, terms_lo = split_pair((0.5 * acoustic) * (jnp.log(prec) - scaled * mean))
    ones = jnp.ones((16, width), jnp.bfloat16)
    contract = (((1,), (1,)), ((), ()))
    offset = lax.dot_general(ones, terms_hi, contract, preferred_element_type=jnp.float32)
    offset = offset + lax.dot_general(
        ones, terms_lo, contract, preferred_element_type=jnp.float32
    )
    offset_hi, offset_lo = split_pair(offset)
    send[half : half + 16, 0:half] = offset_hi
    send[half : half + 16, half : 2 * half] = offset_lo

    straight = trans[...]
    turned_0 = trans[:, 0:half].T
    turned_1 = trans[:, half : 2 * half].T
    base = 4 * width

    @pl.when(core == 0)
    def _():
        keep_t[...] = straight
        send[0:half, base : base + half] = turned_0
        send[0:half, base + half : base + 2 * half] = turned_1

    @pl.when(core == 1)
    def _():
        send[0:half, base : base + 2 * half] = straight
        keep_t[:, 0:half] = turned_0
        keep_t[:, half : 2 * half] = turned_1


def chain_kernel(own_pack, halo_pack, own_w, own_t, other_w, out, x_tile, scores, trans, done, chain, ev, place, ordered, sems):
    core = lax.axis_index("state")
    half, states2 = own_t.shape
    states = 2 * half
    pieces = own_pack.shape[0]
    width = 128 * pieces
    rows = 2 * (own_pack.shape[1] - 8)
    frames = rows // 8
    own_rows = rows // 2
    base = 4 * width

    def assemble(index):
        copies = []
        for n, (is_own, src) in enumerate(((True, own_t), (False, other_w))):
            off = 0 if is_own else base
            at = index if is_own else 1 - index
            for piece in range(2):
                part = src.at[0:half, off + piece * half : off + (piece + 1) * half]
                if index == 0:
                    target = trans.at[at * half : (at + 1) * half, piece * half : (piece + 1) * half]
                else:
                    target = trans.at[piece * half : (piece + 1) * half, at * half : (at + 1) * half]
                copies.append(pltpu.make_async_copy(part, target, sems.at[2 * n + piece]))
        return copies

    @pl.when(core == 0)
    def _():
        for copy in assemble(0):
            copy.start()

    @pl.when(core == 1)
    def _():
        for copy in assemble(1):
            copy.start()

    for j in range(frames):
        at = jnp.where(core == 0, j, frames - 1 - j)
        for c in range(pieces):
            cols = slice(128 * c, 128 * c + 128)
            x_tile[8 * j : 8 * j + 4, cols] = halo_pack[c, pl.ds(at, 4, stride=frames), :]
            x_tile[8 * j + 4 : 8 * j + 8, cols] = own_pack[c, pl.ds(at, 4, stride=frames), :]

    lane = lax.broadcasted_iota(jnp.int32, (4, 128), 1)
    flag4 = jnp.where(
        lane < frames,
        halo_pack[0, own_rows + 4 : own_rows + 8, :],
        own_pack[0, own_rows + 4 : own_rows + 8, :],
    )
    flag4 = jnp.where(lane < 2 * frames, flag4, 0.0)
    flag8 = jnp.concatenate([flag4, flag4], axis=0)
    lane8 = lax.broadcasted_iota(jnp.int32, (8, 128), 1)
    part = jnp.where(lane8 < frames, 0, frames)
    inside = lane8 - part
    when = part + jnp.where(core == 0, inside, frames - 1 - inside) + core
    sub8 = lax.broadcasted_iota(jnp.int32, (8, 128), 0)
    for j in range(frames):
        mine = jnp.where(sub8 < 4, j, frames + j)
        starts = jnp.where((flag8 > 0.5) & (when <= mine), when, -1000)
        last = jnp.max(starts.astype(jnp.float32), axis=1, keepdims=True)
        place[8 * j : 8 * j + 8, :] = mine.astype(jnp.float32) - last

    x = x_tile[...]
    x_hi, x_lo = split_pair(x)
    q_hi, q_lo = split_pair(x * x)
    both = jnp.concatenate(
        [jnp.concatenate([q_hi, x_hi], axis=1), jnp.concatenate([q_lo, x_lo], axis=1)], axis=0
    )
    contract = (((1,), (1,)), ((), ()))

    def half_scores(w):
        main = lax.dot_general(
            both, w[0:half, 0 : 2 * width], contract, preferred_element_type=jnp.float32
        )
        rest = lax.dot_general(
            both[0:rows],
            w[0:half, 2 * width : 4 * width],
            contract,
            preferred_element_type=jnp.float32,
        )
        offset = w[half : half + 1, 0:half].astype(jnp.float32) + w[
            half : half + 1, half : 2 * half
        ].astype(jnp.float32)
        return main[0:rows] + (main[rows : 2 * rows] + rest) + offset

    scores[:, pl.ds(pl.multiple_of(core * half, half), half)] = half_scores(own_w)
    scores[:, pl.ds(pl.multiple_of((1 - core) * half, half), half)] = half_scores(other_w)
    s = scores[...]
    emission = jnp.exp(s - jnp.max(s, axis=1, keepdims=True))
    scores[...] = emission

    line = slice(own_rows, own_rows + 1)
    init_parts = [own_pack[c, line, :] for c in range(pieces)]
    init_parts += [halo_pack[c, line, :] for c in range(pieces)]
    init_row = jnp.where(core == 0, jnp.concatenate(init_parts, axis=1), 1.0)
    prior = init_row / jnp.sum(init_row, axis=1, keepdims=True)

    def finish(k, predicted):
        weighted = scores[...] * predicted
        norm = jnp.sum(weighted, axis=1, keepdims=True)
        alpha = weighted * (1.0 / norm)
        mask = place[...] == k.astype(jnp.float32)
        result = jnp.where(core == 0, alpha, predicted)
        for c in range(states // 128):
            at = slice(128 * c, 128 * c + 128)
            done[:, at] = jnp.where(mask, result[:, at], done[:, at])
        ev[...] = jnp.where(mask, jnp.log(norm), ev[...])
        turned = jnp.concatenate(
            [alpha[rows - 4 : rows], alpha[rows - 8 : rows - 4], alpha[0 : rows - 8]], axis=0
        )
        chain[...] = turned.astype(jnp.bfloat16)

    done[...] = jnp.zeros_like(done)
    ev[...] = jnp.zeros_like(ev)
    finish(jnp.int32(0), jnp.broadcast_to(prior, (rows, states)))

    @pl.when(core == 0)
    def _():
        for copy in assemble(0):
            copy.wait()

    @pl.when(core == 1)
    def _():
        for copy in assemble(1):
            copy.wait()

    def step(k, carry):
        finish(k, jnp.dot(chain[...], trans[...], preferred_element_type=jnp.float32))
        return carry

    lax.fori_loop(1, MAXLEN, step, 0)

    for j in range(frames):
        at = jnp.where(core == 0, j, frames - 1 - j)
        for c in range(states // 128):
            cols = slice(128 * c, 128 * c + 128)
            ordered[c, pl.ds(at, 4, stride=frames), :] = done[8 * j + 4 : 8 * j + 8, cols]
        ordered[states // 128, pl.ds(at, 4, stride=frames), :] = ev[8 * j + 4 : 8 * j + 8, :]
    for c in range(states // 128):
        out[:, 128 * c : 128 * c + 128] = ordered[c].astype(jnp.bfloat16)
    ev_hi, ev_lo = split_pair(ordered[states // 128])
    out[:, states : states + 128] = ev_hi
    out[:, states + 128 : states + 256] = ev_lo


def combine_kernel(own, other, posterior, evidence):
    core = lax.axis_index("state")
    streams, frames, half = posterior.shape
    states = 2 * half
    product = own[:, 0:states].astype(jnp.float32) * other[:, 0:states].astype(jnp.float32)
    inverse = 1.0 / jnp.sum(product, axis=1, keepdims=True)
    mine = jnp.where(core == 0, product[:, 0:half], product[:, half:states])
    posterior[...] = (mine * inverse).astype(jnp.bfloat16).reshape(streams, frames, half)

    def pair(ref):
        return ref[:, states : states + 128].astype(jnp.float32) + ref[
            :, states + 128 : states + 256
        ].astype(jnp.float32)

    logs = jnp.where(core == 0, pair(own), pair(other))
    shape = (streams * frames, 128)
    row = lax.broadcasted_iota(jnp.int32, shape, 0)
    lane = lax.broadcasted_iota(jnp.int32, shape, 1)
    kept = jnp.where(row % frames == lane + core * (frames // 2), logs, 0.0)
    for b in range(streams):
        line = jnp.sum(kept[b * frames : (b + 1) * frames], axis=0, keepdims=True)
        evidence[b : b + 1, :] = line[:, 0 : frames // 2]


def whole(count):
    return [pl.BlockSpec(memory_space=VMEM)] * count


def per_device(features, gauss_means, precisions, transitions, initial, reset_flags):
    streams, frames, width = features.shape
    half = gauss_means.shape[0]
    states = transitions.shape[1]
    rows = streams * frames
    blocks = lax.axis_size("tm")
    devices = 2 * blocks
    bf16, f32 = jnp.bfloat16, jnp.float32

    send, keep_t, pack = pl.pallas_call(
        prepare_kernel,
        out_shape=(
            jax.ShapeDtypeStruct((half + 16, 4 * width + states), bf16),
            jax.ShapeDtypeStruct((half, states), bf16),
            jax.ShapeDtypeStruct((width // 128, rows + 8, 128), f32),
        ),
        in_specs=whole(6),
        out_specs=tuple(whole(3)),
        name="prepare",
    )(features.reshape(rows, width), gauss_means, precisions, transitions, initial, reset_flags)

    neighbours = []
    for i in range(blocks):
        before = (2 * i - 1) % devices
        neighbours += [(before, 2 * i), (2 * i, before)]
    halo = lax.ppermute(pack, ("tm", "state"), neighbours)
    other = lax.ppermute(send, "state", [(0, 1), (1, 0)])

    out = pl.pallas_call(
        chain_kernel,
        out_shape=jax.ShapeDtypeStruct((rows, states + 256), bf16),
        in_specs=whole(5),
        out_specs=whole(1)[0],
        scratch_shapes=[
            VMEM((2 * rows, width), f32),
            VMEM((2 * rows, states), f32),
            VMEM((states, states), bf16),
            VMEM((2 * rows, states), f32),
            VMEM((2 * rows, states), bf16),
            VMEM((2 * rows, 128), f32),
            VMEM((2 * rows, 128), f32),
            VMEM((states // 128 + 1, rows, 128), f32),
            pltpu.SemaphoreType.DMA((4,)),
        ],
        name="chain",
    )(pack, halo, send, keep_t, other)

    out_other = lax.ppermute(out, "state", [(0, 1), (1, 0)])
    return pl.pallas_call(
        combine_kernel,
        out_shape=(
            jax.ShapeDtypeStruct((streams, frames, half), bf16),
            jax.ShapeDtypeStruct((streams, frames // 2), f32),
        ),
        in_specs=whole(2),
        out_specs=tuple(whole(2)),
        name="combine",
    )(out, out_other)


def solution(mesh):
    return jax.shard_map(
        per_device,
        mesh=mesh,
        in_specs=(
            P(None, "tm", None),
            P("state", None),
            P("state", None),
            P("state", None),
            P("state"),
            P(None, "tm"),
        ),
        out_specs=(P(None, "tm", "state"), P(None, ("tm", "state"))),
        check_vma=False,
    )
```

```python
import jax
import jax.numpy as jnp
from jax import lax
from jax.experimental import pallas as pl
from jax.experimental.pallas import tpu as pltpu
from jax.sharding import PartitionSpec as P


MAXLEN = 16
acoustic = 0.1
VMEM = pltpu.VMEM
MIB = 1 << 20
CHUNKS = 4
UNROLL = 3
SCALE = 2.0**108
TRANSPOSED = (((1,), (1,)), ((), ()))
bf16, f32 = jnp.bfloat16, jnp.float32


def split_pair(x):
    high = x.astype(bf16)
    return high, (x - high.astype(f32)).astype(bf16)


def weights_kernel(
    feats, means, precs, flags, init, pack, w_send, prec_in, mean_in, flag_in, init_in, sems
):
    half, width = means.shape
    rows = feats.shape[0]
    streams, frames = flags.shape
    step = half // CHUNKS
    pieces = width // 128
    copies = []
    for n in range(CHUNKS):
        at = slice(n * step, (n + 1) * step)
        copies.append(pltpu.make_async_copy(precs.at[at], prec_in.at[at], sems.at[2 * n]))
        copies.append(pltpu.make_async_copy(means.at[at], mean_in.at[at], sems.at[2 * n + 1]))
    for c in range(pieces):
        part = feats.at[:, 128 * c : 128 * c + 128]
        copies.append(
            pltpu.make_async_copy(part, pack.at[c, 0:rows], sems.at[2 * CHUNKS + c])
        )
    copies.append(pltpu.make_async_copy(flags, flag_in, sems.at[2 * CHUNKS + pieces]))
    copies.append(pltpu.make_async_copy(init, init_in, sems.at[2 * CHUNKS + pieces + 1]))
    for copy in copies:
        copy.start()

    ones = jnp.ones((16, width), bf16)
    for n in range(CHUNKS):
        copies[2 * n].wait()
        copies[2 * n + 1].wait()
        r = n * step
        at = slice(r, r + step)
        prec = prec_in[at, :]
        mean = mean_in[at, :]
        scaled = prec * mean
        quad_hi, quad_lo = split_pair((-0.5 * acoustic) * prec)
        lin_hi, lin_lo = split_pair(acoustic * scaled)
        w_send[at, 0:width] = quad_hi
        w_send[at, width : 2 * width] = lin_hi
        w_send[at, 2 * width : 3 * width] = quad_lo
        w_send[at, 3 * width : 4 * width] = lin_lo
        terms_hi, terms_lo = split_pair((0.5 * acoustic) * (jnp.log(prec) - scaled * mean))
        offset = lax.dot_general(ones, terms_hi, TRANSPOSED, preferred_element_type=f32)
        offset = offset + lax.dot_general(ones, terms_lo, TRANSPOSED, preferred_element_type=f32)
        offset_hi, offset_lo = split_pair(offset)
        w_send[half : half + 16, r : r + step] = offset_hi
        w_send[half : half + 16, half + r : half + r + step] = offset_lo
    for copy in copies[2 * CHUNKS :]:
        copy.wait()
    w_send[half : half + 16, 2 * half : 3 * half] = jnp.broadcast_to(
        init_in[...].astype(f32).reshape(1, half), (16, half)
    ).astype(bf16)
    w_send[half : half + 16, 3 * half : 4 * half] = jnp.zeros((16, half), bf16)
    flags_float = flag_in[...].astype(f32)
    pack[0, rows : rows + 8, :] = jnp.zeros((8, 128), f32)
    pack[0, rows + 4 : rows + 4 + streams, 0:frames] = flags_float
    pack[0, rows + 4 : rows + 4 + streams, frames : 2 * frames] = flags_float


def turn_kernel(trans, t_send, t_keep):
    core = lax.axis_index("state")
    half = trans.shape[0]
    turned_0 = trans[:, 0:half].T
    turned_1 = trans[:, half : 2 * half].T

    @pl.when(core == 0)
    def _():
        t_keep[...] = trans[...]
        t_send[:, 0:half] = turned_1
        t_send[:, half : 2 * half] = turned_0

    @pl.when(core == 1)
    def _():
        t_send[...] = trans[...]
        t_keep[:, 0:half] = turned_1
        t_keep[:, half : 2 * half] = turned_0


def half_scores(both, w):
    width = w.shape[1] // 4
    half = w.shape[0] - 16
    rows = both.shape[0] // 2
    main = lax.dot_general(
        both[...], w[0:half, 0 : 2 * width], TRANSPOSED, preferred_element_type=f32
    )
    rest = lax.dot_general(
        both[0:rows, :],
        w[0:half, 2 * width : 4 * width],
        TRANSPOSED,
        preferred_element_type=f32,
    )
    extra = w[half : half + 1, 0 : 2 * half].astype(f32)
    return main[0:rows] + (main[rows : 2 * rows] + rest) + (extra[:, 0:half] + extra[:, half:])


def scores_kernel(own_pack, halo_pack, own_w, both, scores, place):
    core = lax.axis_index("state")
    is_last = lax.axis_index("tm") == lax.axis_size("tm") - 1
    pieces = own_pack.shape[0]
    width = 128 * pieces
    own_rows = own_pack.shape[1] - 8
    rows = 2 * own_rows
    frames = rows // 8

    lane = lax.broadcasted_iota(jnp.int32, (4, 128), 1)
    end_reset = jnp.where((core == 1) & is_last, 1.0, 0.0)
    flag4 = jnp.where(
        lane < frames,
        jnp.maximum(halo_pack[0, own_rows + 4 : own_rows + 8, :], end_reset),
        own_pack[0, own_rows + 4 : own_rows + 8, :],
    )
    flag4 = jnp.where(lane < 2 * frames, flag4, 0.0)
    flag8 = jnp.concatenate([flag4, flag4], axis=0)
    lane8 = lax.broadcasted_iota(jnp.int32, (8, 128), 1)
    part = jnp.where(lane8 < frames, 0, frames)
    inside = lane8 - part
    when = part + jnp.where(core == 0, inside, frames - 1 - inside) + core
    sub8 = lax.broadcasted_iota(jnp.int32, (8, 128), 0)
    for j in range(frames):
        mine = jnp.where(sub8 < 4, j, frames + j)
        starts = jnp.where((flag8 > 0.5) & (when <= mine), when, -1000)
        last = jnp.max(starts.astype(f32), axis=1, keepdims=True)
        place[8 * j : 8 * j + 8, :] = mine.astype(f32) - last

    for c in range(pieces):
        tiles = []
        for j in range(frames):
            at = jnp.where(core == 0, j, frames - 1 - j)
            tiles.append(halo_pack[c, pl.ds(at, 4, stride=frames), :])
            tiles.append(own_pack[c, pl.ds(at, 4, stride=frames), :])
        x = jnp.concatenate(tiles, axis=0)
        x_hi, x_lo = split_pair(x)
        q_hi, q_lo = split_pair(x * x)
        cols = slice(128 * c, 128 * c + 128)
        past = slice(width + 128 * c, width + 128 * c + 128)
        both[0:rows, cols] = q_hi
        both[0:rows, past] = x_hi
        both[rows : 2 * rows, cols] = q_lo
        both[rows : 2 * rows, past] = x_lo
    scores[...] = half_scores(both, own_w)


def emission_kernel(both, own_scores, other_w, emission):
    half = own_scores.shape[1]
    other_scores = half_scores(both, other_w)
    mine = own_scores[...]
    top = jnp.maximum(
        jnp.max(mine, axis=1, keepdims=True), jnp.max(other_scores, axis=1, keepdims=True)
    )
    emission[:, 0:half] = jnp.exp(mine - top)
    emission[:, half : 2 * half] = jnp.exp(other_scores - top)


def chain_kernel(
    emission, place, own_w, other_w, own_t, other_t, out, chain, done, part, gain, sums, gains, ordered
):
    core = lax.axis_index("state")
    half, states = own_t.shape
    rows = place.shape[0]
    frames = rows // 8
    shape = (rows, 128)

    def advance(x):
        last = x[rows - 8 : rows]
        return jnp.concatenate([last[4:8], last[0:4], x[0 : rows - 8]], axis=0)

    def settle(k):
        total = jnp.broadcast_to(jnp.sum(part[...], axis=1, keepdims=True) * gain[...], shape)
        sums[...] = jnp.where(place[...] == k - 1.0, total, sums[...])
        return total

    def spread(k, predicted, scale, index):
        mask = place[...] == k
        sum_tile = None
        for c in range(states // 128):
            at = slice(128 * c, 128 * c + 128)
            ahead = predicted[:, at]
            weighted = ahead * emission[:, at]
            sum_tile = weighted if sum_tile is None else sum_tile + weighted
            result = weighted if index == 0 else ahead
            done[:, at] = jnp.where(mask, result, done[:, at])
            chain[:, at] = advance(weighted * scale).astype(bf16)
        part[...] = sum_tile

    def run(index):
        if index == 0:
            line = slice(half, half + 1)
            first = jnp.concatenate(
                [w[line, 2 * half : 3 * half].astype(f32) for w in (own_w, other_w)], axis=1
            )
            first = first / jnp.sum(first, axis=1, keepdims=True)
        else:
            first = jnp.full((1, states), 1.0 / states, f32)
        gain[...] = jnp.full(shape, SCALE, f32)
        gains[...] = jnp.full(shape, SCALE, f32)
        sums[...] = jnp.full(shape, SCALE, f32)
        done[...] = jnp.zeros_like(done)
        spread(0.0, jnp.broadcast_to(first, (rows, states)), SCALE, index)

        def step(k, carry):
            k = k.astype(f32)
            total = settle(k)
            scale = SCALE / advance(total)
            gain[...] = scale
            gains[...] = jnp.where(place[...] == k, scale, gains[...])
            mine, theirs = chain[:, 0:half], chain[:, half:states]
            if index == 0:
                blocks = (own_t[:, 0:half], other_t[:, 0:half], own_t[:, half:], other_t[:, half:])
            else:
                blocks = (own_t[:, 0:half], own_t[:, half:], other_t[:, 0:half], other_t[:, half:])
            predicted = jnp.concatenate(
                [
                    jnp.dot(mine, blocks[2 * n], preferred_element_type=f32)
                    + jnp.dot(theirs, blocks[2 * n + 1], preferred_element_type=f32)
                    for n in range(2)
                ],
                axis=1,
            )
            spread(k, predicted, scale, index)
            return carry

        lax.fori_loop(1, MAXLEN, step, 0, unroll=UNROLL)
        settle(float(MAXLEN))
        norm = sums[...]
        scale = gains[...] / norm if index == 0 else gains[...] * (1.0 / SCALE)
        logs = jnp.log(norm * (1.0 / SCALE))
        last = states // 128
        for j in range(frames):
            at = j if index == 0 else frames - 1 - j
            own = slice(8 * j + 4, 8 * j + 8)
            for c in range(last):
                cols = slice(128 * c, 128 * c + 128)
                ordered[c, pl.ds(at, 4, stride=frames), :] = done[own, cols] * scale[own]
            ordered[last, pl.ds(at, 4, stride=frames), :] = logs[own]
        for c in range(last):
            out[:, 128 * c : 128 * c + 128] = ordered[c].astype(bf16)
        logs_hi, logs_lo = split_pair(ordered[last])
        out[:, states : states + 128] = logs_hi
        out[:, states + 128 : states + 256] = logs_lo

    for index in range(2):

        @pl.when(core == index)
        def _():
            run(index)


def combine_kernel(own, other, posterior, evidence):
    core = lax.axis_index("state")
    streams, frames, half = posterior.shape
    states = 2 * half
    mine = own[:, 0:half].astype(f32) * other[:, half:states].astype(f32)
    theirs = own[:, half:states].astype(f32) * other[:, 0:half].astype(f32)
    inverse = 1.0 / jnp.sum(mine + theirs, axis=1, keepdims=True)
    posterior[...] = (mine * inverse).astype(bf16).reshape(streams, frames, half)

    def pair(ref):
        return ref[:, states : states + 128].astype(f32) + ref[
            :, states + 128 : states + 256
        ].astype(f32)

    logs = jnp.where(core == 0, pair(own), pair(other))
    shape = (streams * frames, 128)
    row = lax.broadcasted_iota(jnp.int32, shape, 0)
    lane = lax.broadcasted_iota(jnp.int32, shape, 1)
    kept = jnp.where(row % frames == lane + core * (frames // 2), logs, 0.0)
    for b in range(streams):
        line = jnp.sum(kept[b * frames : (b + 1) * frames], axis=0, keepdims=True)
        evidence[b : b + 1, :] = line[:, 0 : frames // 2]


def kernel(body, outs, scratch, vmem, cost, *args, hbm=()):
    in_vmem = pl.BlockSpec(memory_space=VMEM)
    in_hbm = pl.BlockSpec(memory_space=pltpu.HBM)
    args = [
        pltpu.with_memory_space_constraint(a, pltpu.HBM) if n in hbm else a
        for n, a in enumerate(args)
    ]
    return pl.pallas_call(
        body,
        out_shape=[jax.ShapeDtypeStruct(*o) for o in outs],
        in_specs=[in_hbm if n in hbm else in_vmem for n in range(len(args))],
        out_specs=[in_vmem] * len(outs),
        scratch_shapes=scratch,
        compiler_params=pltpu.CompilerParams(vmem_limit_bytes=vmem * MIB),
        cost_estimate=pl.CostEstimate(flops=cost, bytes_accessed=1 * MIB, transcendentals=0),
    )(*args)


def per_device(features, gauss_means, precisions, transitions, initial, reset_flags):
    streams, frames, width = features.shape
    half = gauss_means.shape[0]
    states = transitions.shape[1]
    rows = streams * frames
    blocks = lax.axis_size("tm")
    partner = [(0, 1), (1, 0)]

    pack, w_send = kernel(
        weights_kernel,
        [((width // 128, rows + 8, 128), f32), ((half + 16, 4 * width), bf16)],
        [
            VMEM((half, width), f32),
            VMEM((half, width), f32),
            VMEM((streams, frames), jnp.int32),
            VMEM((half,), bf16),
            pltpu.SemaphoreType.DMA((2 * CHUNKS + width // 128 + 2,)),
        ],
        16, 10**9,
        features.reshape(rows, width), gauss_means, precisions, reset_flags, initial,
        hbm=range(5),
    )
    pairs = [(2 * i - 1, 2 * i) for i in range(1, blocks)]
    halo = lax.ppermute(pack, ("tm", "state"), pairs + [(b, a) for a, b in pairs])
    other_w = lax.ppermute(w_send, "state", partner)
    t_send, t_keep = kernel(
        turn_kernel,
        [((half, states), bf16), ((half, states), bf16)],
        [], 16, 10**9,
        transitions,
    )
    other_t = lax.ppermute(t_send, "state", partner)
    both, scores, place = kernel(
        scores_kernel,
        [((4 * rows, 2 * width), bf16), ((2 * rows, half), f32), ((2 * rows, 128), f32)],
        [], 16, 10**9,
        pack, halo, w_send,
    )
    (emission,) = kernel(
        emission_kernel, [((2 * rows, states), f32)], [], 16, 10**9,
        both, scores, other_w,
    )
    wide, narrow = VMEM((2 * rows, states), f32), VMEM((2 * rows, 128), f32)
    (out,) = kernel(
        chain_kernel,
        [((rows, states + 256), bf16)],
        [
            VMEM((2 * rows, states), bf16),
            wide, narrow, narrow, narrow, narrow,
            VMEM((states // 128 + 1, rows, 128), f32),
        ],
        24, 10**10,
        emission, place, w_send, other_w, t_keep, other_t,
    )
    out_other = lax.ppermute(out, "state", partner)
    posterior, evidence = kernel(
        combine_kernel,
        [((streams, frames, half), bf16), ((streams, frames // 2), f32)],
        [], 8, 10**6,
        out, out_other,
    )
    return posterior, evidence


def solution(mesh):
    return jax.shard_map(
        per_device,
        mesh=mesh,
        in_specs=(
            P(None, "tm", None),
            P("state", None),
            P("state", None),
            P("state", None),
            P("state"),
            P(None, "tm"),
        ),
        out_specs=(P(None, "tm", "state"), P(None, ("tm", "state"))),
        check_vma=False,
    )
```

```python
import jax
import jax.numpy as jnp
from jax import lax
from jax.experimental import pallas as pl
from jax.experimental.pallas import tpu as pltpu
from jax.sharding import PartitionSpec as P


MAXLEN = 16
acoustic = 0.1
VMEM = pltpu.VMEM
MIB = 1 << 20
UNROLL = 3
PARTS = 1
SCALE = 2.0**108
TRANSPOSED = (((1,), (1,)), ((), ()))
bf16, f32 = jnp.bfloat16, jnp.float32


def split_pair(x):
    high = x.astype(bf16)
    return high, (x - high.astype(f32)).astype(bf16)


def pair_columns(x):
    x_hi, x_lo = split_pair(x)
    q_hi, q_lo = split_pair(x * x)
    high = jnp.concatenate([q_hi, x_hi], axis=1)
    return jnp.concatenate([high, jnp.concatenate([q_lo, x_lo], axis=1)], axis=0)


def some_scores(both, w_hi, w_lo, offset):
    rows = both.shape[0] // 2
    main = lax.dot_general(both, w_hi, TRANSPOSED, preferred_element_type=f32)
    rest = lax.dot_general(both[0:rows], w_lo, TRANSPOSED, preferred_element_type=f32)
    return main[0:rows] + (main[rows:] + rest) + offset


def front_kernel(
    feats, means, precs, flags, init, pack, w, offsets,
    x_in, prec_in, mean_in, flag_in, init_in, sems,
):
    half, width = means.shape
    rows = feats.shape[0]
    streams, frames = flags.shape
    pieces = width // 128
    pairs = [(feats, x_in)]
    for n in range(PARTS):
        at = slice(n * half // PARTS, (n + 1) * half // PARTS)
        pairs += [(precs.at[at], prec_in.at[at]), (means.at[at], mean_in.at[at])]
    pairs += [(flags, flag_in), (init, init_in)]
    copies = [pltpu.make_async_copy(*p, sems.at[n]) for n, p in enumerate(pairs)]
    for copy in copies:
        copy.start()
    for n in (0, -2, -1):
        copies[n].wait()
    x = x_in[...]
    for c in range(pieces):
        pack[c, 0:rows, :] = x[:, 128 * c : 128 * c + 128]
    init_row = init_in[...].astype(f32).reshape(1, half)
    for c in range(pieces):
        pack[c, 2 * rows : 2 * rows + 8, :] = jnp.broadcast_to(
            init_row[:, 128 * c : 128 * c + 128], (8, 128)
        )
    flags_float = flag_in[...].astype(f32)
    pack[0, 2 * rows + 4 : 2 * rows + 4 + streams, 0:frames] = flags_float
    pack[0, 2 * rows + 4 : 2 * rows + 4 + streams, frames : 2 * frames] = flags_float
    both = pair_columns(x)
    ones = jnp.ones((16, 128), bf16)

    def prepare(n):
        at = slice(n * 128, n * 128 + 128)
        prec = prec_in[at, :]
        mean = mean_in[at, :]
        scaled = prec * mean
        quad_hi, quad_lo = split_pair((-0.5 * acoustic) * prec)
        lin_hi, lin_lo = split_pair(acoustic * scaled)
        w_hi = jnp.concatenate([quad_hi, lin_hi], axis=1)
        w_lo = jnp.concatenate([quad_lo, lin_lo], axis=1)
        w[at, 0 : 2 * width] = w_hi
        w[at, 2 * width : 4 * width] = w_lo
        squares = scaled * mean
        product, total, logs = None, None, None
        for c in range(pieces):
            cols = slice(128 * c, 128 * c + 128)
            product = prec[:, cols] if product is None else product * prec[:, cols]
            total = squares[:, cols] if total is None else total + squares[:, cols]
            if c % 4 == 3 or c == pieces - 1:
                logs = jnp.log(product) if logs is None else logs + jnp.log(product)
                product = None
        return w_hi, w_lo, split_pair((0.5 * acoustic) * (logs - total))

    def score(n, w_hi, w_lo, terms):
        offset = sum(
            lax.dot_general(ones, t, TRANSPOSED, preferred_element_type=f32) for t in terms
        )
        offsets[:, n * 128 : n * 128 + 128] = offset[0:8]
        pack[n, rows : 2 * rows, :] = some_scores(both, w_hi, w_lo, offset[0:1])

    tiles = half // 128
    for part in range(PARTS):
        copies[1 + 2 * part].wait()
        copies[2 + 2 * part].wait()
        for n in range(part * tiles // PARTS, (part + 1) * tiles // PARTS):
            score(n, *prepare(n))


def turn_kernel(own_t, other_t, own_turned, other_turned):
    half = own_t.shape[0]

    @pl.when(lax.axis_index("state") == 1)
    def _():
        for source, target in ((own_t, own_turned), (other_t, other_turned)):
            target[:, 0:half] = source[:, half : 2 * half].T
            target[:, half : 2 * half] = source[:, 0:half].T


def halo_kernel(own_pack, halo_pack, w, offsets, halo_scores, place):
    core = lax.axis_index("state")
    is_last = lax.axis_index("tm") == lax.axis_size("tm") - 1
    pieces = own_pack.shape[0]
    width = 128 * pieces
    half = w.shape[0]
    rows = (own_pack.shape[1] - 8) // 2
    frames = rows // 4

    x = jnp.concatenate([halo_pack[c, 0:rows, :] for c in range(pieces)], axis=1)
    computed = some_scores(
        pair_columns(x), w[:, 0 : 2 * width], w[:, 2 * width : 4 * width], offsets[0:1, :]
    )
    for c in range(half // 128):
        halo_scores[c, :, :] = computed[:, 128 * c : 128 * c + 128]

    lane = lax.broadcasted_iota(jnp.int32, (4, 128), 1)
    end_reset = jnp.where((core == 1) & is_last, 1.0, 0.0)
    flag_rows = slice(2 * rows + 4, 2 * rows + 8)
    flag4 = jnp.where(
        lane < frames,
        jnp.maximum(halo_pack[0, flag_rows, :], end_reset),
        own_pack[0, flag_rows, :],
    )
    flag4 = jnp.where(lane < 2 * frames, flag4, 0.0)
    flag8 = jnp.concatenate([flag4, flag4], axis=0)
    lane8 = lax.broadcasted_iota(jnp.int32, (8, 128), 1)
    part = jnp.where(lane8 < frames, 0, frames)
    inside = lane8 - part
    when = part + jnp.where(core == 0, inside, frames - 1 - inside) + core
    sub8 = lax.broadcasted_iota(jnp.int32, (8, 128), 0)
    for j in range(frames):
        mine = jnp.where(sub8 < 4, j, frames + j)
        starts = jnp.where((flag8 > 0.5) & (when <= mine), when, -1000)
        last = jnp.max(starts.astype(f32), axis=1, keepdims=True)
        place[8 * j : 8 * j + 8, :] = mine.astype(f32) - last


def emission_kernel(own_pack, halo_pack, pair_pack, halo_scores, emission):
    core = lax.axis_index("state")
    rows = halo_scores.shape[1]
    half = 128 * halo_scores.shape[0]
    frames = rows // 4
    for j in range(frames):
        at = jnp.where(core == 0, j, frames - 1 - j)
        tiles = []
        for near, far, first in ((halo_scores, own_pack, 0), (halo_pack, pair_pack, rows)):
            for c in range(half // 128):
                before = near[c, pl.ds(at + first, 4, stride=frames), :]
                now = far[c, pl.ds(at + rows, 4, stride=frames), :]
                tiles.append(jnp.concatenate([before, now], axis=0))
        top = tiles[0]
        for tile in tiles[1:]:
            top = jnp.maximum(top, tile)
        top = jnp.max(top, axis=1, keepdims=True)
        for c, tile in enumerate(tiles):
            emission[8 * j : 8 * j + 8, 128 * c : 128 * c + 128] = jnp.exp(tile - top)


def chain_kernel(
    emission, place, own_pack, pair_pack, own_t, other_t, own_turned, other_turned,
    out, chain, done, part, gain, sums, gains, ordered,
):
    core = lax.axis_index("state")
    half, states = own_t.shape
    rows = place.shape[0]
    frames = rows // 8
    shape = (rows, 128)

    def advance(x):
        last = x[rows - 8 : rows]
        return jnp.concatenate([last[4:8], last[0:4], x[0 : rows - 8]], axis=0)

    def settle(k):
        total = jnp.broadcast_to(jnp.sum(part[...], axis=1, keepdims=True) * gain[...], shape)
        sums[...] = jnp.where(place[...] == k - 1.0, total, sums[...])
        return total

    def spread(k, predicted, scale, index):
        mask = place[...] == k
        sum_tile = None
        for c in range(states // 128):
            at = slice(128 * c, 128 * c + 128)
            ahead = predicted[:, at]
            weighted = ahead * emission[:, at]
            sum_tile = weighted if sum_tile is None else sum_tile + weighted
            result = weighted if index == 0 else ahead
            done[:, at] = jnp.where(mask, result, done[:, at])
            chain[:, at] = advance(weighted * scale).astype(bf16)
        part[...] = sum_tile

    def run(index):
        if index == 0:
            line = slice(own_pack.shape[1] - 8, own_pack.shape[1] - 7)
            first = jnp.concatenate(
                [p[c, line, :] for p in (own_pack, pair_pack) for c in range(half // 128)], axis=1
            )
            first = first / jnp.sum(first, axis=1, keepdims=True)
        else:
            first = jnp.full((1, states), 1.0 / states, f32)
        gain[...] = jnp.full(shape, SCALE, f32)
        gains[...] = jnp.full(shape, SCALE, f32)
        sums[...] = jnp.full(shape, SCALE, f32)
        done[...] = jnp.zeros_like(done)
        spread(0.0, jnp.broadcast_to(first, (rows, states)), SCALE, index)

        def step(k, carry):
            k = k.astype(f32)
            total = settle(k)
            scale = SCALE / advance(total)
            gain[...] = scale
            gains[...] = jnp.where(place[...] == k, scale, gains[...])
            mine, theirs = chain[:, 0:half], chain[:, half:states]
            if index == 0:
                blocks = (own_t[:, 0:half], other_t[:, 0:half], own_t[:, half:], other_t[:, half:])
            else:
                mine_t, other = own_turned, other_turned
                blocks = (mine_t[:, 0:half], mine_t[:, half:], other[:, 0:half], other[:, half:])
            predicted = jnp.concatenate(
                [
                    jnp.dot(mine, blocks[2 * n], preferred_element_type=f32)
                    + jnp.dot(theirs, blocks[2 * n + 1], preferred_element_type=f32)
                    for n in range(2)
                ],
                axis=1,
            )
            spread(k, predicted, scale, index)
            return carry

        lax.fori_loop(1, MAXLEN, step, 0, unroll=UNROLL)
        settle(float(MAXLEN))
        norm = sums[...]
        scale = gains[...] / norm if index == 0 else gains[...] * (1.0 / SCALE)
        logs = jnp.log(norm * (1.0 / SCALE))
        last = states // 128
        for j in range(frames):
            at = j if index == 0 else frames - 1 - j
            own = slice(8 * j + 4, 8 * j + 8)
            for c in range(last):
                cols = slice(128 * c, 128 * c + 128)
                ordered[c, pl.ds(at, 4, stride=frames), :] = done[own, cols] * scale[own]
            ordered[last, pl.ds(at, 4, stride=frames), :] = logs[own]
        for c in range(last):
            out[:, 128 * c : 128 * c + 128] = ordered[c].astype(bf16)
        logs_hi, logs_lo = split_pair(ordered[last])
        out[:, states : states + 128] = logs_hi
        out[:, states + 128 : states + 256] = logs_lo

    for index in range(2):

        @pl.when(core == index)
        def _():
            run(index)


def combine_kernel(own, other, posterior, evidence):
    core = lax.axis_index("state")
    streams, frames, half = posterior.shape
    states = 2 * half
    mine = own[:, 0:half].astype(f32) * other[:, half:states].astype(f32)
    theirs = own[:, half:states].astype(f32) * other[:, 0:half].astype(f32)
    inverse = 1.0 / jnp.sum(mine + theirs, axis=1, keepdims=True)
    posterior[...] = (mine * inverse).astype(bf16).reshape(streams, frames, half)

    def pair(ref):
        return ref[:, states : states + 128].astype(f32) + ref[
            :, states + 128 : states + 256
        ].astype(f32)

    logs = jnp.where(core == 0, pair(own), pair(other))
    shape = (streams * frames, 128)
    row = lax.broadcasted_iota(jnp.int32, shape, 0)
    lane = lax.broadcasted_iota(jnp.int32, shape, 1)
    kept = jnp.where(row % frames == lane + core * (frames // 2), logs, 0.0)
    for b in range(streams):
        line = jnp.sum(kept[b * frames : (b + 1) * frames], axis=0, keepdims=True)
        evidence[b : b + 1, :] = line[:, 0 : frames // 2]


def kernel(body, outs, scratch, vmem, cost, *args, hbm=()):
    in_vmem = pl.BlockSpec(memory_space=VMEM)
    in_hbm = pl.BlockSpec(memory_space=pltpu.HBM)
    args = [
        pltpu.with_memory_space_constraint(a, pltpu.HBM) if n in hbm else a
        for n, a in enumerate(args)
    ]
    return pl.pallas_call(
        body,
        out_shape=[jax.ShapeDtypeStruct(*o) for o in outs],
        in_specs=[in_hbm if n in hbm else in_vmem for n in range(len(args))],
        out_specs=[in_vmem] * len(outs),
        scratch_shapes=scratch,
        compiler_params=pltpu.CompilerParams(vmem_limit_bytes=vmem * MIB),
        cost_estimate=pl.CostEstimate(flops=cost, bytes_accessed=1 * MIB, transcendentals=0),
    )(*args)


def per_device(features, gauss_means, precisions, transitions, initial, reset_flags):
    streams, frames, width = features.shape
    half = gauss_means.shape[0]
    states = transitions.shape[1]
    rows = streams * frames
    blocks = lax.axis_size("tm")
    partner = [(0, 1), (1, 0)]

    pack, w, offsets = kernel(
        front_kernel,
        [((width // 128, 2 * rows + 8, 128), f32), ((half, 4 * width), bf16), ((8, half), f32)],
        [
            VMEM((rows, width), f32),
            VMEM((half, width), f32),
            VMEM((half, width), f32),
            VMEM((streams, frames), jnp.int32),
            VMEM((half,), bf16),
            pltpu.SemaphoreType.DMA((2 * PARTS + 3,)),
        ],
        16, 10**9,
        features.reshape(rows, width), gauss_means, precisions, reset_flags, initial,
        hbm=range(5),
    )
    pairs = [(2 * i - 1, 2 * i) for i in range(1, blocks)]
    halo = lax.ppermute(pack, ("tm", "state"), pairs + [(b, a) for a, b in pairs])
    other_t = lax.ppermute(transitions, "state", partner)
    pair = lax.ppermute(pack, "state", partner)
    own_turned, other_turned = kernel(
        turn_kernel,
        [((half, states), bf16), ((half, states), bf16)],
        [], 16, 10**9,
        transitions, other_t,
    )
    halo_scores, place = kernel(
        halo_kernel,
        [((half // 128, rows, 128), f32), ((2 * rows, 128), f32)],
        [], 16, 10**9,
        pack, halo, w, offsets,
    )
    (emission,) = kernel(
        emission_kernel, [((2 * rows, states), f32)], [], 16, 10**9,
        pack, halo, pair, halo_scores,
    )
    wide, narrow = VMEM((2 * rows, states), f32), VMEM((2 * rows, 128), f32)
    (out,) = kernel(
        chain_kernel,
        [((rows, states + 256), bf16)],
        [
            VMEM((2 * rows, states), bf16),
            wide, narrow, narrow, narrow, narrow,
            VMEM((states // 128 + 1, rows, 128), f32),
        ],
        24, 10**10,
        emission, place, pack, pair, transitions, other_t, own_turned, other_turned,
    )
    out_other = lax.ppermute(out, "state", partner)
    posterior, evidence = kernel(
        combine_kernel,
        [((streams, frames, half), bf16), ((streams, frames // 2), f32)],
        [], 8, 10**6,
        out, out_other,
    )
    return posterior, evidence


def solution(mesh):
    return jax.shard_map(
        per_device,
        mesh=mesh,
        in_specs=(
            P(None, "tm", None),
            P("state", None),
            P("state", None),
            P("state", None),
            P("state"),
            P(None, "tm"),
        ),
        out_specs=(P(None, "tm", "state"), P(None, ("tm", "state"))),
        check_vma=False,
    )
```

```python
import jax
import jax.numpy as jnp
from jax import lax
from jax.experimental import pallas as pl
from jax.experimental.pallas import tpu as pltpu
from jax.sharding import PartitionSpec as P


MAXLEN = 16
acoustic = 0.1
VMEM = pltpu.VMEM
MIB = 1 << 20
UNROLL = 3
PARTS = 1
SCALE = 2.0**108
TRANSPOSED = (((1,), (1,)), ((), ()))
bf16, f32 = jnp.bfloat16, jnp.float32


def split_pair(x):
    high = x.astype(bf16)
    return high, (x - high.astype(f32)).astype(bf16)


def pair_columns(x):
    x_hi, x_lo = split_pair(x)
    q_hi, q_lo = split_pair(x * x)
    high = jnp.concatenate([q_hi, x_hi], axis=1)
    return jnp.concatenate([high, jnp.concatenate([q_lo, x_lo], axis=1)], axis=0)


def some_scores(both, w_hi, w_lo, offset):
    rows = both.shape[0] // 2
    main = jnp.dot(both, w_hi, preferred_element_type=f32)
    rest = jnp.dot(both[0:rows], w_lo, preferred_element_type=f32)
    return main[0:rows] + (main[rows:] + rest) + offset


def front_kernel(
    feats, means, precs, flags, init, pack, scored, w, offsets,
    extra, x_in, prec_in, mean_in, flag_in, init_in, sems,
):
    half, width = means.shape
    rows = feats.shape[0]
    streams, frames = flags.shape
    pieces = width // 128
    pairs = [(feats, x_in)]
    for n in range(PARTS):
        at = slice(n * half // PARTS, (n + 1) * half // PARTS)
        pairs += [(precs.at[at], prec_in.at[at]), (means.at[at], mean_in.at[at])]
    pairs += [(flags, flag_in), (init, init_in)]
    copies = [pltpu.make_async_copy(*p, sems.at[n]) for n, p in enumerate(pairs)]
    for copy in copies:
        copy.start()
    for n in (0, -2, -1):
        copies[n].wait()
    init_row = init_in[...].astype(f32).reshape(1, half)
    for c in range(half // 128):
        scored[c, rows : rows + 8, :] = jnp.broadcast_to(
            init_row[:, 128 * c : 128 * c + 128], (8, 128)
        )
    both = pair_columns(x_in[...])
    pack[:, 0:width] = both[0:rows, width : 2 * width]
    pack[:, width : 2 * width] = both[rows : 2 * rows, width : 2 * width]
    ones = jnp.ones((16, 128), bf16)

    def prepare(n):
        at = slice(n * 128, n * 128 + 128)
        prec = prec_in[at, :]
        mean = mean_in[at, :]
        scaled = prec * mean
        quad_hi, quad_lo = split_pair((-0.5 * acoustic) * prec)
        lin_hi, lin_lo = split_pair(acoustic * scaled)
        w_hi = jnp.concatenate([quad_hi.T, lin_hi.T], axis=0)
        w_lo = jnp.concatenate([quad_lo.T, lin_lo.T], axis=0)
        w[:, at] = w_hi
        w[:, half + n * 128 : half + n * 128 + 128] = w_lo
        squares = scaled * mean
        product, total, logs = None, None, None
        for c in range(pieces):
            cols = slice(128 * c, 128 * c + 128)
            product = prec[:, cols] if product is None else product * prec[:, cols]
            total = squares[:, cols] if total is None else total + squares[:, cols]
            if c % 4 == 3 or c == pieces - 1:
                logs = jnp.log(product) if logs is None else logs + jnp.log(product)
                product = None
        return w_hi, w_lo, split_pair((0.5 * acoustic) * (logs - total))

    def score(n, w_hi, w_lo, terms):
        offset = sum(
            lax.dot_general(ones, t, TRANSPOSED, preferred_element_type=f32) for t in terms
        )
        offsets[:, n * 128 : n * 128 + 128] = offset[0:8]
        scored[n, 0:rows, :] = some_scores(both, w_hi, w_lo, offset[0:1])

    tiles = half // 128
    for part in range(PARTS):
        copies[1 + 2 * part].wait()
        copies[2 + 2 * part].wait()
        for n in range(part * tiles // PARTS, (part + 1) * tiles // PARTS):
            score(n, *prepare(n))

    top = scored[0, 0:rows, :]
    for c in range(1, tiles):
        top = jnp.maximum(top, scored[c, 0:rows, :])
    top = jnp.max(top, axis=1, keepdims=True)
    for c in range(tiles):
        at = slice(2 * width + 128 * c, 2 * width + 128 * c + 128)
        pack[:, at] = jnp.exp(scored[c, 0:rows, :] - top).astype(bf16)
    extra[...] = jnp.zeros_like(extra)
    flags_float = flag_in[...].astype(f32)
    for b in range(streams):
        line = jnp.broadcast_to(flags_float[b : b + 1, :], (frames, frames))
        extra[b * frames : (b + 1) * frames, 0:frames] = line
        extra[b * frames : (b + 1) * frames, frames : 2 * frames] = line
    top_hi = top.astype(bf16)
    extra[:, 2 * frames : 2 * frames + 1] = top_hi.astype(f32)
    rest = top - top_hi.astype(f32)
    rest_hi, rest_lo = split_pair(rest)
    extra[:, 2 * frames + 1 : 2 * frames + 2] = rest_hi.astype(f32)
    extra[:, 2 * frames + 2 : 2 * frames + 3] = rest_lo.astype(f32)
    pack[:, 2 * width + half : 2 * width + half + 128] = extra[...].astype(bf16)


def turn_kernel(own_t, other_t, own_turned, other_turned):
    half = own_t.shape[0]

    @pl.when(lax.axis_index("state") == 1)
    def _():
        for source, target in ((own_t, own_turned), (other_t, other_turned)):
            target[:, 0:half] = source[:, half : 2 * half].T
            target[:, half : 2 * half] = source[:, 0:half].T


def halo_kernel(own_pack, halo_pack, w, offsets, halo_scores, far_scores, place):
    core = lax.axis_index("state")
    is_last = lax.axis_index("tm") == lax.axis_size("tm") - 1
    width = w.shape[0] // 2
    half = w.shape[1] // 2
    rows = own_pack.shape[0]
    frames = rows // 4
    side = slice(2 * width + half, 2 * width + half + 128)

    x_hi, x_lo = halo_pack[:, 0:width], halo_pack[:, width : 2 * width]
    x = x_hi.astype(f32) + x_lo.astype(f32)
    q_hi, q_lo = split_pair(x * x)
    both = jnp.concatenate(
        [jnp.concatenate([q_hi, x_hi], axis=1), jnp.concatenate([q_lo, x_lo], axis=1)], axis=0
    )
    computed = some_scores(both, w[:, 0:half], w[:, half : 2 * half], offsets[0:1, :])
    halo_side = halo_pack[:, side].astype(f32)
    own_side = own_pack[:, side].astype(f32)
    spot = lax.broadcasted_iota(jnp.int32, (rows, 128), 1) - 2 * frames
    top = jnp.sum(jnp.where((spot >= 0) & (spot < 3), halo_side, 0.0), axis=1, keepdims=True)
    for c in range(half // 128):
        at = slice(128 * c, 128 * c + 128)
        halo_scores[c, :, :] = computed[:, at]
        sent = halo_pack[:, 2 * width + 128 * c : 2 * width + 128 * c + 128].astype(f32)
        far_scores[c, :, :] = top + jnp.log(sent)

    lane = lax.broadcasted_iota(jnp.int32, (4, 128), 1)
    end_reset = jnp.where((core == 1) & is_last, 1.0, 0.0)
    halo_flags = jnp.concatenate([halo_side[b : b + 1] for b in range(0, rows, frames)], axis=0)
    own_flags = jnp.concatenate([own_side[b : b + 1] for b in range(0, rows, frames)], axis=0)
    flag4 = jnp.where(lane < frames, jnp.maximum(halo_flags, end_reset), own_flags)
    flag4 = jnp.where(lane < 2 * frames, flag4, 0.0)
    flag8 = jnp.concatenate([flag4, flag4], axis=0)
    lane8 = lax.broadcasted_iota(jnp.int32, (8, 128), 1)
    part = jnp.where(lane8 < frames, 0, frames)
    inside = lane8 - part
    when = part + jnp.where(core == 0, inside, frames - 1 - inside) + core
    sub8 = lax.broadcasted_iota(jnp.int32, (8, 128), 0)
    for j in range(frames):
        mine = jnp.where(sub8 < 4, j, frames + j)
        starts = jnp.where((flag8 > 0.5) & (when <= mine), when, -1000)
        last = jnp.max(starts.astype(f32), axis=1, keepdims=True)
        place[8 * j : 8 * j + 8, :] = mine.astype(f32) - last


def emission_kernel(own_scores, far_scores, pair_scores, halo_scores, emission):
    core = lax.axis_index("state")
    rows = halo_scores.shape[1]
    half = 128 * halo_scores.shape[0]
    frames = rows // 4
    for j in range(frames):
        at = jnp.where(core == 0, j, frames - 1 - j)
        tiles = []
        for near, far in ((halo_scores, own_scores), (far_scores, pair_scores)):
            for c in range(half // 128):
                before = near[c, pl.ds(at, 4, stride=frames), :]
                now = far[c, pl.ds(at, 4, stride=frames), :]
                tiles.append(jnp.concatenate([before, now], axis=0))
        top = tiles[0]
        for tile in tiles[1:]:
            top = jnp.maximum(top, tile)
        top = jnp.max(top, axis=1, keepdims=True)
        for c, tile in enumerate(tiles):
            emission[8 * j : 8 * j + 8, 128 * c : 128 * c + 128] = jnp.exp(tile - top)


def chain_kernel(
    emission, place, own_scores, pair_scores, own_t, other_t, own_turned, other_turned,
    out, chain, done, part, gain, sums, gains, ordered,
):
    core = lax.axis_index("state")
    half, states = own_t.shape
    rows = place.shape[0]
    frames = rows // 8
    own_rows = rows // 2
    shape = (rows, 128)

    def advance(x):
        last = x[rows - 8 : rows]
        return jnp.concatenate([last[4:8], last[0:4], x[0 : rows - 8]], axis=0)

    def settle(k):
        total = jnp.broadcast_to(jnp.sum(part[...], axis=1, keepdims=True) * gain[...], shape)
        sums[...] = jnp.where(place[...] == k - 1.0, total, sums[...])
        return total

    def spread(k, predicted, scale, index):
        mask = place[...] == k
        sum_tile = None
        for c in range(states // 128):
            at = slice(128 * c, 128 * c + 128)
            ahead = predicted[:, at]
            weighted = ahead * emission[:, at]
            sum_tile = weighted if sum_tile is None else sum_tile + weighted
            result = weighted if index == 0 else ahead
            done[:, at] = jnp.where(mask, result, done[:, at])
            chain[:, at] = advance(weighted * scale).astype(bf16)
        part[...] = sum_tile

    def run(index):
        if index == 0:
            line = slice(own_rows, own_rows + 1)
            first = jnp.concatenate(
                [p[c, line, :] for p in (own_scores, pair_scores) for c in range(half // 128)], axis=1
            )
            first = first / jnp.sum(first, axis=1, keepdims=True)
        else:
            first = jnp.full((1, states), 1.0 / states, f32)
        gain[...] = jnp.full(shape, SCALE, f32)
        gains[...] = jnp.full(shape, SCALE, f32)
        sums[...] = jnp.full(shape, SCALE, f32)
        done[...] = jnp.zeros_like(done)
        spread(0.0, jnp.broadcast_to(first, (rows, states)), SCALE, index)

        def step(k, carry):
            k = k.astype(f32)
            total = settle(k)
            scale = SCALE / advance(total)
            gain[...] = scale
            gains[...] = jnp.where(place[...] == k, scale, gains[...])
            mine, theirs = chain[:, 0:half], chain[:, half:states]
            if index == 0:
                blocks = (own_t[:, 0:half], other_t[:, 0:half], own_t[:, half:], other_t[:, half:])
            else:
                mine_t, other = own_turned, other_turned
                blocks = (mine_t[:, 0:half], mine_t[:, half:], other[:, 0:half], other[:, half:])
            predicted = jnp.concatenate(
                [
                    jnp.dot(mine, blocks[2 * n], preferred_element_type=f32)
                    + jnp.dot(theirs, blocks[2 * n + 1], preferred_element_type=f32)
                    for n in range(2)
                ],
                axis=1,
            )
            spread(k, predicted, scale, index)
            return carry

        lax.fori_loop(1, MAXLEN, step, 0, unroll=UNROLL)
        settle(float(MAXLEN))
        norm = sums[...]
        scale = gains[...] / norm if index == 0 else gains[...] * (1.0 / SCALE)
        logs = jnp.log(norm * (1.0 / SCALE))
        last = states // 128
        for j in range(frames):
            at = j if index == 0 else frames - 1 - j
            own = slice(8 * j + 4, 8 * j + 8)
            for c in range(last):
                cols = slice(128 * c, 128 * c + 128)
                ordered[c, pl.ds(at, 4, stride=frames), :] = done[own, cols] * scale[own]
            ordered[last, pl.ds(at, 4, stride=frames), :] = logs[own]
        for c in range(last):
            out[:, 128 * c : 128 * c + 128] = ordered[c].astype(bf16)
        logs_hi, logs_lo = split_pair(ordered[last])
        out[:, states : states + 128] = logs_hi
        out[:, states + 128 : states + 256] = logs_lo

    for index in range(2):

        @pl.when(core == index)
        def _():
            run(index)


def combine_kernel(own, other, posterior, evidence):
    core = lax.axis_index("state")
    streams, frames, half = posterior.shape
    states = 2 * half
    mine = own[:, 0:half].astype(f32) * other[:, half:states].astype(f32)
    theirs = own[:, half:states].astype(f32) * other[:, 0:half].astype(f32)
    inverse = 1.0 / jnp.sum(mine + theirs, axis=1, keepdims=True)
    posterior[...] = (mine * inverse).astype(bf16).reshape(streams, frames, half)

    def pair(ref):
        return ref[:, states : states + 128].astype(f32) + ref[
            :, states + 128 : states + 256
        ].astype(f32)

    logs = jnp.where(core == 0, pair(own), pair(other))
    shape = (streams * frames, 128)
    row = lax.broadcasted_iota(jnp.int32, shape, 0)
    lane = lax.broadcasted_iota(jnp.int32, shape, 1)
    kept = jnp.where(row % frames == lane + core * (frames // 2), logs, 0.0)
    for b in range(streams):
        line = jnp.sum(kept[b * frames : (b + 1) * frames], axis=0, keepdims=True)
        evidence[b : b + 1, :] = line[:, 0 : frames // 2]


def kernel(body, outs, scratch, vmem, cost, *args, hbm=()):
    in_vmem = pl.BlockSpec(memory_space=VMEM)
    in_hbm = pl.BlockSpec(memory_space=pltpu.HBM)
    args = [
        pltpu.with_memory_space_constraint(a, pltpu.HBM) if n in hbm else a
        for n, a in enumerate(args)
    ]
    return pl.pallas_call(
        body,
        out_shape=[jax.ShapeDtypeStruct(*o) for o in outs],
        in_specs=[in_hbm if n in hbm else in_vmem for n in range(len(args))],
        out_specs=[in_vmem] * len(outs),
        scratch_shapes=scratch,
        compiler_params=pltpu.CompilerParams(vmem_limit_bytes=vmem * MIB),
        cost_estimate=pl.CostEstimate(flops=cost, bytes_accessed=1 * MIB, transcendentals=0),
    )(*args)


def per_device(features, gauss_means, precisions, transitions, initial, reset_flags):
    streams, frames, width = features.shape
    half = gauss_means.shape[0]
    states = transitions.shape[1]
    rows = streams * frames
    blocks = lax.axis_size("tm")
    partner = [(0, 1), (1, 0)]

    pack, scored, w, offsets = kernel(
        front_kernel,
        [
            ((rows, 2 * width + half + 128), bf16),
            ((half // 128, rows + 8, 128), f32),
            ((2 * width, 2 * half), bf16),
            ((8, half), f32),
        ],
        [
            VMEM((rows, 128), f32),
            VMEM((rows, width), f32),
            VMEM((half, width), f32),
            VMEM((half, width), f32),
            VMEM((streams, frames), jnp.int32),
            VMEM((half,), bf16),
            pltpu.SemaphoreType.DMA((2 * PARTS + 3,)),
        ],
        16, 10**9,
        features.reshape(rows, width), gauss_means, precisions, reset_flags, initial,
        hbm=range(5),
    )
    pairs = [(2 * i - 1, 2 * i) for i in range(1, blocks)]
    halo = lax.ppermute(pack, ("tm", "state"), pairs + [(b, a) for a, b in pairs])
    other_t = lax.ppermute(transitions, "state", partner)
    pair = lax.ppermute(scored, "state", partner)
    own_turned, other_turned = kernel(
        turn_kernel,
        [((half, states), bf16), ((half, states), bf16)],
        [], 16, 10**9,
        transitions, other_t,
    )
    halo_scores, far_scores, place = kernel(
        halo_kernel,
        [((half // 128, rows, 128), f32)] * 2 + [((2 * rows, 128), f32)],
        [], 16, 10**9,
        pack, halo, w, offsets,
    )
    (emission,) = kernel(
        emission_kernel, [((2 * rows, states), f32)], [], 16, 10**9,
        scored, far_scores, pair, halo_scores,
    )
    wide, narrow = VMEM((2 * rows, states), f32), VMEM((2 * rows, 128), f32)
    (out,) = kernel(
        chain_kernel,
        [((rows, states + 256), bf16)],
        [
            VMEM((2 * rows, states), bf16),
            wide, narrow, narrow, narrow, narrow,
            VMEM((states // 128 + 1, rows, 128), f32),
        ],
        24, 10**10,
        emission, place, scored, pair, transitions, other_t, own_turned, other_turned,
    )
    out_other = lax.ppermute(out, "state", partner)
    posterior, evidence = kernel(
        combine_kernel,
        [((streams, frames, half), bf16), ((streams, frames // 2), f32)],
        [], 8, 10**6,
        out, out_other,
    )
    return posterior, evidence


def solution(mesh):
    return jax.shard_map(
        per_device,
        mesh=mesh,
        in_specs=(
            P(None, "tm", None),
            P("state", None),
            P("state", None),
            P("state", None),
            P("state"),
            P(None, "tm"),
        ),
        out_specs=(P(None, "tm", "state"), P(None, ("tm", "state"))),
        check_vma=False,
    )
```

```python
import jax
import jax.numpy as jnp
from jax import lax
from jax.experimental import pallas as pl
from jax.experimental.pallas import tpu as pltpu
from jax.sharding import PartitionSpec as P


MAXLEN = 16
acoustic = 0.1
VMEM = pltpu.VMEM
MIB = 1 << 20
UNROLL = 3
PARTS = 2
SCALE = 2.0**108
TRANSPOSED = (((1,), (1,)), ((), ()))
bf16, f32 = jnp.bfloat16, jnp.float32


def split_pair(x):
    high = x.astype(bf16)
    return high, (x - high.astype(f32)).astype(bf16)


def pair_columns(x_hi, x_lo):
    x = x_hi.astype(f32) + x_lo.astype(f32)
    q_hi, q_lo = split_pair((-0.5 / acoustic) * (x * x))
    high = jnp.concatenate([q_hi, x_hi], axis=1)
    return jnp.concatenate([high, jnp.concatenate([q_lo, x_lo], axis=1)], axis=0)


def some_scores(both, w_hi, w_lo, offset):
    rows = both.shape[0] // 2
    main = jnp.dot(both, w_hi, preferred_element_type=f32)
    rest = jnp.dot(both[0:rows], w_lo, preferred_element_type=f32)
    return main[0:rows] + (main[rows:] + rest) + offset


def front_kernel(
    feats, means, precs, flags, init, pack, scored, w, offsets,
    extra, x_in, prec_in, mean_in, flag_in, init_in, sems,
):
    half, width = means.shape
    rows = feats.shape[0]
    streams, frames = flags.shape
    pieces = width // 128
    pairs = [(feats, x_in)]
    for n in range(PARTS):
        at = slice(n * half // PARTS, (n + 1) * half // PARTS)
        pairs += [(precs.at[at], prec_in.at[at]), (means.at[at], mean_in.at[at])]
    pairs += [(flags, flag_in), (init, init_in)]
    copies = [pltpu.make_async_copy(*p, sems.at[n]) for n, p in enumerate(pairs)]
    for copy in copies:
        copy.start()
    for n in (0, -2, -1):
        copies[n].wait()
    init_row = init_in[...].astype(f32).reshape(1, half)
    for c in range(half // 128):
        scored[c, rows : rows + 8, :] = jnp.broadcast_to(
            init_row[:, 128 * c : 128 * c + 128], (8, 128)
        )
    x_hi, x_lo = split_pair(acoustic * x_in[...])
    pack[:, 0:width] = x_hi
    pack[:, width : 2 * width] = x_lo
    both = pair_columns(x_hi, x_lo)
    ones = jnp.ones((16, 128), bf16)

    def prepare(n):
        at = slice(n * 128, n * 128 + 128)
        prec = prec_in[at, :]
        mean = mean_in[at, :]
        scaled = prec * mean
        quad_hi, quad_lo = split_pair(prec)
        lin_hi, lin_lo = split_pair(scaled)
        w_hi = jnp.concatenate([quad_hi.T, lin_hi.T], axis=0)
        w_lo = jnp.concatenate([quad_lo.T, lin_lo.T], axis=0)
        w[:, at] = w_hi
        w[:, half + n * 128 : half + n * 128 + 128] = w_lo
        squares = scaled * mean
        product, total, logs = None, None, None
        for c in range(pieces):
            cols = slice(128 * c, 128 * c + 128)
            product = prec[:, cols] if product is None else product * prec[:, cols]
            total = squares[:, cols] if total is None else total + squares[:, cols]
            if c % 4 == 3 or c == pieces - 1:
                logs = jnp.log(product) if logs is None else logs + jnp.log(product)
                product = None
        return w_hi, w_lo, split_pair((0.5 * acoustic) * (logs - total))

    def score(n, w_hi, w_lo, terms):
        offset = sum(
            lax.dot_general(ones, t, TRANSPOSED, preferred_element_type=f32) for t in terms
        )
        offsets[:, n * 128 : n * 128 + 128] = offset[0:8]
        scored[n, 0:rows, :] = some_scores(both, w_hi, w_lo, offset[0:1])

    tiles = half // 128
    for part in range(PARTS):
        copies[1 + 2 * part].wait()
        copies[2 + 2 * part].wait()
        for n in range(part * tiles // PARTS, (part + 1) * tiles // PARTS):
            score(n, *prepare(n))

    top = scored[0, 0:rows, :]
    for c in range(1, tiles):
        top = jnp.maximum(top, scored[c, 0:rows, :])
    top = jnp.max(top, axis=1, keepdims=True)
    for c in range(tiles):
        at = slice(2 * width + 128 * c, 2 * width + 128 * c + 128)
        pack[:, at] = jnp.exp(scored[c, 0:rows, :] - top).astype(bf16)
    extra[...] = jnp.zeros_like(extra)
    flags_float = flag_in[...].astype(f32)
    for b in range(streams):
        line = jnp.broadcast_to(flags_float[b : b + 1, :], (frames, frames))
        extra[b * frames : (b + 1) * frames, 0:frames] = line
        extra[b * frames : (b + 1) * frames, frames : 2 * frames] = line
    top_hi = top.astype(bf16)
    extra[:, 2 * frames : 2 * frames + 1] = top_hi.astype(f32)
    rest = top - top_hi.astype(f32)
    rest_hi, rest_lo = split_pair(rest)
    extra[:, 2 * frames + 1 : 2 * frames + 2] = rest_hi.astype(f32)
    extra[:, 2 * frames + 2 : 2 * frames + 3] = rest_lo.astype(f32)
    pack[:, 2 * width + half : 2 * width + half + 128] = extra[...].astype(bf16)


def turn_kernel(source, turned):
    half = source.shape[0]

    @pl.when(lax.axis_index("state") == 1)
    def _():
        turned[:, 0:half] = source[:, half : 2 * half].T
        turned[:, half : 2 * half] = source[:, 0:half].T


def halo_kernel(own_pack, halo_pack, w, offsets, halo_scores, far_scores, place):
    core = lax.axis_index("state")
    is_last = lax.axis_index("tm") == lax.axis_size("tm") - 1
    width = w.shape[0] // 2
    half = w.shape[1] // 2
    rows = own_pack.shape[0]
    frames = rows // 4
    side = slice(2 * width + half, 2 * width + half + 128)

    both = pair_columns(halo_pack[:, 0:width], halo_pack[:, width : 2 * width])
    computed = some_scores(both, w[:, 0:half], w[:, half : 2 * half], offsets[0:1, :])
    halo_side = halo_pack[:, side].astype(f32)
    own_side = own_pack[:, side].astype(f32)
    spot = lax.broadcasted_iota(jnp.int32, (rows, 128), 1) - 2 * frames
    top = jnp.sum(jnp.where((spot >= 0) & (spot < 3), halo_side, 0.0), axis=1, keepdims=True)
    for c in range(half // 128):
        at = slice(128 * c, 128 * c + 128)
        halo_scores[c, :, :] = computed[:, at]
        sent = halo_pack[:, 2 * width + 128 * c : 2 * width + 128 * c + 128].astype(f32)
        far_scores[c, :, :] = top + jnp.log(sent)

    lane = lax.broadcasted_iota(jnp.int32, (4, 128), 1)
    end_reset = jnp.where((core == 1) & is_last, 1.0, 0.0)
    halo_flags = jnp.concatenate([halo_side[b : b + 1] for b in range(0, rows, frames)], axis=0)
    own_flags = jnp.concatenate([own_side[b : b + 1] for b in range(0, rows, frames)], axis=0)
    flag4 = jnp.where(lane < frames, jnp.maximum(halo_flags, end_reset), own_flags)
    flag4 = jnp.where(lane < 2 * frames, flag4, 0.0)
    flag8 = jnp.concatenate([flag4, flag4], axis=0)
    lane8 = lax.broadcasted_iota(jnp.int32, (8, 128), 1)
    part = jnp.where(lane8 < frames, 0, frames)
    inside = lane8 - part
    when = part + jnp.where(core == 0, inside, frames - 1 - inside) + core
    sub8 = lax.broadcasted_iota(jnp.int32, (8, 128), 0)
    for j in range(frames):
        mine = jnp.where(sub8 < 4, j, frames + j)
        starts = jnp.where((flag8 > 0.5) & (when <= mine), when, -1000)
        last = jnp.max(starts.astype(f32), axis=1, keepdims=True)
        place[8 * j : 8 * j + 8, :] = mine.astype(f32) - last


def emission_kernel(own_scores, far_scores, pair_scores, halo_scores, emission):
    core = lax.axis_index("state")
    rows = halo_scores.shape[1]
    half = 128 * halo_scores.shape[0]
    frames = rows // 4
    for j in range(frames):
        at = jnp.where(core == 0, j, frames - 1 - j)
        tiles = []
        for near, far in ((halo_scores, own_scores), (far_scores, pair_scores)):
            for c in range(half // 128):
                before = near[c, pl.ds(at, 4, stride=frames), :]
                now = far[c, pl.ds(at, 4, stride=frames), :]
                tiles.append(jnp.concatenate([before, now], axis=0))
        top = tiles[0]
        for tile in tiles[1:]:
            top = jnp.maximum(top, tile)
        top = jnp.max(top, axis=1, keepdims=True)
        for c, tile in enumerate(tiles):
            emission[8 * j : 8 * j + 8, 128 * c : 128 * c + 128] = jnp.exp(tile - top)


def chain_kernel(
    emission, place, own_scores, pair_scores, own_t, other_t, own_turned, other_turned,
    out, chain, done, part, gain, sums, gains, ordered,
):
    core = lax.axis_index("state")
    half, states = own_t.shape
    rows = place.shape[0]
    frames = rows // 8
    own_rows = rows // 2
    shape = (rows, 128)

    def advance(x):
        last = x[rows - 8 : rows]
        return jnp.concatenate([last[4:8], last[0:4], x[0 : rows - 8]], axis=0)

    def settle(k):
        total = jnp.broadcast_to(jnp.sum(part[...], axis=1, keepdims=True) * gain[...], shape)
        sums[...] = jnp.where(place[...] == k - 1.0, total, sums[...])
        return total

    def spread(k, predicted, scale, index, first=False):
        mask = place[...] == k
        sum_tile = None
        for c in range(states // 128):
            at = slice(128 * c, 128 * c + 128)
            ahead = predicted[:, at]
            weighted = ahead * emission[:, at]
            sum_tile = weighted if sum_tile is None else sum_tile + weighted
            result = weighted if index == 0 else ahead
            done[:, at] = result if first else jnp.where(mask, result, done[:, at])
            chain[:, at] = advance(weighted * scale).astype(bf16)
        part[...] = sum_tile

    def run(index):
        if index == 0:
            line = slice(own_rows, own_rows + 1)
            first = jnp.concatenate(
                [p[c, line, :] for p in (own_scores, pair_scores) for c in range(half // 128)], axis=1
            )
            first = first / jnp.sum(first, axis=1, keepdims=True)
        else:
            first = jnp.full((1, states), 1.0 / states, f32)
        gain[...] = jnp.full(shape, SCALE, f32)
        gains[...] = jnp.full(shape, SCALE, f32)
        sums[...] = jnp.full(shape, SCALE, f32)
        spread(0.0, jnp.broadcast_to(first, (rows, states)), SCALE, index, True)

        def step(k, carry):
            k = k.astype(f32)
            total = settle(k)
            scale = SCALE / advance(total)
            gain[...] = scale
            gains[...] = jnp.where(place[...] == k, scale, gains[...])
            mine, theirs = chain[:, 0:half], chain[:, half:states]
            if index == 0:
                blocks = (own_t[:, 0:half], other_t[:, 0:half], own_t[:, half:], other_t[:, half:])
            else:
                mine_t, other = own_turned, other_turned
                blocks = (mine_t[:, 0:half], mine_t[:, half:], other[:, 0:half], other[:, half:])
            predicted = jnp.concatenate(
                [
                    jnp.dot(mine, blocks[2 * n], preferred_element_type=f32)
                    + jnp.dot(theirs, blocks[2 * n + 1], preferred_element_type=f32)
                    for n in range(2)
                ],
                axis=1,
            )
            spread(k, predicted, scale, index)
            return carry

        lax.fori_loop(1, MAXLEN, step, 0, unroll=UNROLL)
        settle(float(MAXLEN))
        norm = sums[...]
        scale = gains[...] / norm if index == 0 else gains[...] * (1.0 / SCALE)
        logs = jnp.log(norm * (1.0 / SCALE))
        last = states // 128
        for j in range(frames):
            at = j if index == 0 else frames - 1 - j
            own = slice(8 * j + 4, 8 * j + 8)
            for c in range(last):
                cols = slice(128 * c, 128 * c + 128)
                ordered[c, pl.ds(at, 4, stride=frames), :] = done[own, cols] * scale[own]
            ordered[last, pl.ds(at, 4, stride=frames), :] = logs[own]
        for c in range(last):
            out[:, 128 * c : 128 * c + 128] = ordered[c].astype(bf16)
        logs_hi, logs_lo = split_pair(ordered[last])
        out[:, states : states + 128] = logs_hi
        out[:, states + 128 : states + 256] = logs_lo

    for index in range(2):

        @pl.when(core == index)
        def _():
            run(index)


def combine_kernel(own, other, posterior, evidence):
    core = lax.axis_index("state")
    streams, frames, half = posterior.shape
    states = 2 * half
    mine = own[:, 0:half].astype(f32) * other[:, half:states].astype(f32)
    theirs = own[:, half:states].astype(f32) * other[:, 0:half].astype(f32)
    inverse = 1.0 / jnp.sum(mine + theirs, axis=1, keepdims=True)
    posterior[...] = (mine * inverse).astype(bf16).reshape(streams, frames, half)

    def pair(ref):
        return ref[:, states : states + 128].astype(f32) + ref[
            :, states + 128 : states + 256
        ].astype(f32)

    logs = jnp.where(core == 0, pair(own), pair(other))
    shape = (streams * frames, 128)
    row = lax.broadcasted_iota(jnp.int32, shape, 0)
    lane = lax.broadcasted_iota(jnp.int32, shape, 1)
    kept = jnp.where(row % frames == lane + core * (frames // 2), logs, 0.0)
    for b in range(streams):
        line = jnp.sum(kept[b * frames : (b + 1) * frames], axis=0, keepdims=True)
        evidence[b : b + 1, :] = line[:, 0 : frames // 2]


def kernel(body, outs, scratch, vmem, cost, *args, hbm=()):
    in_vmem = pl.BlockSpec(memory_space=VMEM)
    in_hbm = pl.BlockSpec(memory_space=pltpu.HBM)
    args = [
        pltpu.with_memory_space_constraint(a, pltpu.HBM) if n in hbm else a
        for n, a in enumerate(args)
    ]
    return pl.pallas_call(
        body,
        out_shape=[jax.ShapeDtypeStruct(*o) for o in outs],
        in_specs=[in_hbm if n in hbm else in_vmem for n in range(len(args))],
        out_specs=[in_vmem] * len(outs),
        scratch_shapes=scratch,
        compiler_params=pltpu.CompilerParams(vmem_limit_bytes=vmem * MIB),
        cost_estimate=pl.CostEstimate(flops=cost, bytes_accessed=1 * MIB, transcendentals=0),
    )(*args)


def per_device(features, gauss_means, precisions, transitions, initial, reset_flags):
    streams, frames, width = features.shape
    half = gauss_means.shape[0]
    states = transitions.shape[1]
    rows = streams * frames
    blocks = lax.axis_size("tm")
    partner = [(0, 1), (1, 0)]

    pack, scored, w, offsets = kernel(
        front_kernel,
        [
            ((rows, 2 * width + half + 128), bf16),
            ((half // 128, rows + 8, 128), f32),
            ((2 * width, 2 * half), bf16),
            ((8, half), f32),
        ],
        [
            VMEM((rows, 128), f32),
            VMEM((rows, width), f32),
            VMEM((half, width), f32),
            VMEM((half, width), f32),
            VMEM((streams, frames), jnp.int32),
            VMEM((half,), bf16),
            pltpu.SemaphoreType.DMA((2 * PARTS + 3,)),
        ],
        16, 10**9,
        features.reshape(rows, width), gauss_means, precisions, reset_flags, initial,
        hbm=range(5),
    )
    pairs = [(2 * i - 1, 2 * i) for i in range(1, blocks)]
    halo = lax.ppermute(pack, ("tm", "state"), pairs + [(b, a) for a, b in pairs])
    other_t = lax.ppermute(transitions, "state", partner)
    pair = lax.ppermute(scored, "state", partner)
    block = [((half, states), bf16)]
    (own_turned,) = kernel(turn_kernel, block, [], 16, 10**9, transitions)
    (other_turned,) = kernel(turn_kernel, block, [], 16, 10**9, other_t)
    halo_scores, far_scores, place = kernel(
        halo_kernel,
        [((half // 128, rows, 128), f32)] * 2 + [((2 * rows, 128), f32)],
        [], 16, 10**9,
        pack, halo, w, offsets,
    )
    (emission,) = kernel(
        emission_kernel, [((2 * rows, states), f32)], [], 16, 10**9,
        scored, far_scores, pair, halo_scores,
    )
    wide, narrow = VMEM((2 * rows, states), f32), VMEM((2 * rows, 128), f32)
    (out,) = kernel(
        chain_kernel,
        [((rows, states + 256), bf16)],
        [
            VMEM((2 * rows, states), bf16),
            wide, narrow, narrow, narrow, narrow,
            VMEM((states // 128 + 1, rows, 128), f32),
        ],
        24, 10**10,
        emission, place, scored, pair, transitions, other_t, own_turned, other_turned,
    )
    out_other = lax.ppermute(out, "state", partner)
    posterior, evidence = kernel(
        combine_kernel,
        [((streams, frames, half), bf16), ((streams, frames // 2), f32)],
        [], 8, 10**6,
        out, out_other,
    )
    return posterior, evidence


def solution(mesh):
    return jax.shard_map(
        per_device,
        mesh=mesh,
        in_specs=(
            P(None, "tm", None),
            P("state", None),
            P("state", None),
            P("state", None),
            P("state"),
            P(None, "tm"),
        ),
        out_specs=(P(None, "tm", "state"), P(None, ("tm", "state"))),
        check_vma=False,
    )
```

```python
import jax
import jax.numpy as jnp
from jax import lax
from jax.experimental import pallas as pl
from jax.experimental.pallas import tpu as pltpu
from jax.sharding import PartitionSpec as P


MAXLEN = 16
acoustic = 0.1
VMEM = pltpu.VMEM
MIB = 1 << 20
UNROLL = 15
PARTS = 2
SCALE = 2.0**108
TRANSPOSED = (((1,), (1,)), ((), ()))
bf16, f32 = jnp.bfloat16, jnp.float32


def split_pair(x):
    high = x.astype(bf16)
    return high, (x - high.astype(f32)).astype(bf16)


def pair_columns(x_hi, x_lo):
    x = x_hi.astype(f32) + x_lo.astype(f32)
    q_hi, q_lo = split_pair((-0.5 / acoustic) * (x * x))
    high = jnp.concatenate([q_hi, x_hi], axis=1)
    return jnp.concatenate([high, jnp.concatenate([q_lo, x_lo], axis=1)], axis=0)


def some_scores(both, w_hi, w_lo, offset):
    rows = both.shape[0] // 2
    main = jnp.dot(both, w_hi, preferred_element_type=f32)
    rest = jnp.dot(both[0:rows], w_lo, preferred_element_type=f32)
    return main[0:rows] + (main[rows:] + rest) + offset


def front_kernel(
    feats, means, precs, flags, init, pack, scored, w, offsets,
    extra, x_in, prec_in, mean_in, flag_in, init_in, sems,
):
    half, width = means.shape
    rows = feats.shape[0]
    streams, frames = flags.shape
    pieces = width // 128
    pairs = [(feats, x_in), (flags, flag_in), (init, init_in)]
    for n in range(PARTS):
        at = slice(n * half // PARTS, (n + 1) * half // PARTS)
        pairs += [(precs.at[at], prec_in.at[at]), (means.at[at], mean_in.at[at])]
    copies = [pltpu.make_async_copy(*p, sems.at[n]) for n, p in enumerate(pairs)]
    for copy in copies:
        copy.start()
    copies[0].wait()
    x_hi, x_lo = split_pair(acoustic * x_in[...])
    pack[:, 0:width] = x_hi
    pack[:, width : 2 * width] = x_lo
    both = pair_columns(x_hi, x_lo)
    ones = jnp.ones((16, 128), bf16)

    def prepare(n):
        at = slice(n * 128, n * 128 + 128)
        prec = prec_in[at, :]
        mean = mean_in[at, :]
        scaled = prec * mean
        quad_hi, quad_lo = split_pair(prec)
        lin_hi, lin_lo = split_pair(scaled)
        w_hi = jnp.concatenate([quad_hi.T, lin_hi.T], axis=0)
        w_lo = jnp.concatenate([quad_lo.T, lin_lo.T], axis=0)
        w[:, at] = w_hi
        w[:, half + n * 128 : half + n * 128 + 128] = w_lo
        squares = scaled * mean
        product, total, logs = None, None, None
        for c in range(pieces):
            cols = slice(128 * c, 128 * c + 128)
            product = prec[:, cols] if product is None else product * prec[:, cols]
            total = squares[:, cols] if total is None else total + squares[:, cols]
            if c % 4 == 3 or c == pieces - 1:
                logs = jnp.log(product) if logs is None else logs + jnp.log(product)
                product = None
        return w_hi, w_lo, split_pair((0.5 * acoustic) * (logs - total))

    def score(n, w_hi, w_lo, terms):
        offset = sum(
            lax.dot_general(ones, t, TRANSPOSED, preferred_element_type=f32) for t in terms
        )
        offsets[:, n * 128 : n * 128 + 128] = offset[0:8]
        scored[n, 0:rows, :] = some_scores(both, w_hi, w_lo, offset[0:1])

    tiles = half // 128
    for part in range(PARTS):
        copies[3 + 2 * part].wait()
        copies[4 + 2 * part].wait()
        for n in range(part * tiles // PARTS, (part + 1) * tiles // PARTS):
            score(n, *prepare(n))

    copies[1].wait()
    copies[2].wait()
    init_row = init_in[...].astype(f32).reshape(1, half)
    for c in range(half // 128):
        scored[c, rows : rows + 8, :] = jnp.broadcast_to(
            init_row[:, 128 * c : 128 * c + 128], (8, 128)
        )

    top = scored[0, 0:rows, :]
    for c in range(1, tiles):
        top = jnp.maximum(top, scored[c, 0:rows, :])
    top = jnp.max(top, axis=1, keepdims=True)
    for c in range(tiles):
        at = slice(2 * width + 128 * c, 2 * width + 128 * c + 128)
        pack[:, at] = jnp.exp(scored[c, 0:rows, :] - top).astype(bf16)
    extra[...] = jnp.zeros_like(extra)
    flags_float = flag_in[...].astype(f32)
    for b in range(streams):
        line = jnp.broadcast_to(flags_float[b : b + 1, :], (frames, frames))
        extra[b * frames : (b + 1) * frames, 0:frames] = line
        extra[b * frames : (b + 1) * frames, frames : 2 * frames] = line
    top_hi = top.astype(bf16)
    extra[:, 2 * frames : 2 * frames + 1] = top_hi.astype(f32)
    rest = top - top_hi.astype(f32)
    rest_hi, rest_lo = split_pair(rest)
    extra[:, 2 * frames + 1 : 2 * frames + 2] = rest_hi.astype(f32)
    extra[:, 2 * frames + 2 : 2 * frames + 3] = rest_lo.astype(f32)
    pack[:, 2 * width + half : 2 * width + half + 128] = extra[...].astype(bf16)


def turn_kernel(source, turned):
    half = source.shape[0]

    @pl.when(lax.axis_index("state") == 1)
    def _():
        turned[:, 0:half] = source[:, half : 2 * half].T
        turned[:, half : 2 * half] = source[:, 0:half].T


def halo_kernel(own_pack, halo_pack, w, offsets, halo_scores, far_scores, place):
    core = lax.axis_index("state")
    is_last = lax.axis_index("tm") == lax.axis_size("tm") - 1
    width = w.shape[0] // 2
    half = w.shape[1] // 2
    rows = own_pack.shape[0]
    frames = rows // 4
    side = slice(2 * width + half, 2 * width + half + 128)

    both = pair_columns(halo_pack[:, 0:width], halo_pack[:, width : 2 * width])
    computed = some_scores(both, w[:, 0:half], w[:, half : 2 * half], offsets[0:1, :])
    halo_side = halo_pack[:, side].astype(f32)
    own_side = own_pack[:, side].astype(f32)
    spot = lax.broadcasted_iota(jnp.int32, (rows, 128), 1) - 2 * frames
    top = jnp.sum(jnp.where((spot >= 0) & (spot < 3), halo_side, 0.0), axis=1, keepdims=True)
    for c in range(half // 128):
        at = slice(128 * c, 128 * c + 128)
        halo_scores[c, :, :] = computed[:, at]
        sent = halo_pack[:, 2 * width + 128 * c : 2 * width + 128 * c + 128].astype(f32)
        far_scores[c, :, :] = top + jnp.log(sent)

    lane = lax.broadcasted_iota(jnp.int32, (4, 128), 1)
    end_reset = jnp.where((core == 1) & is_last, 1.0, 0.0)
    halo_flags = jnp.concatenate([halo_side[b : b + 1] for b in range(0, rows, frames)], axis=0)
    own_flags = jnp.concatenate([own_side[b : b + 1] for b in range(0, rows, frames)], axis=0)
    flag4 = jnp.where(lane < frames, jnp.maximum(halo_flags, end_reset), own_flags)
    flag4 = jnp.where(lane < 2 * frames, flag4, 0.0)
    flag8 = jnp.concatenate([flag4, flag4], axis=0)
    lane8 = lax.broadcasted_iota(jnp.int32, (8, 128), 1)
    part = jnp.where(lane8 < frames, 0, frames)
    inside = lane8 - part
    when = part + jnp.where(core == 0, inside, frames - 1 - inside) + core
    sub8 = lax.broadcasted_iota(jnp.int32, (8, 128), 0)
    for j in range(frames):
        mine = jnp.where(sub8 < 4, j, frames + j)
        starts = jnp.where((flag8 > 0.5) & (when <= mine), when, -1000)
        last = jnp.max(starts.astype(f32), axis=1, keepdims=True)
        place[8 * j : 8 * j + 8, :] = mine.astype(f32) - last


def emission_kernel(own_scores, far_scores, pair_scores, halo_scores, emission):
    core = lax.axis_index("state")
    rows = halo_scores.shape[1]
    half = 128 * halo_scores.shape[0]
    frames = rows // 4
    for j in range(frames):
        at = jnp.where(core == 0, j, frames - 1 - j)
        tiles = []
        for near, far in ((halo_scores, own_scores), (far_scores, pair_scores)):
            for c in range(half // 128):
                before = near[c, pl.ds(at, 4, stride=frames), :]
                now = far[c, pl.ds(at, 4, stride=frames), :]
                tiles.append(jnp.concatenate([before, now], axis=0))
        top = tiles[0]
        for tile in tiles[1:]:
            top = jnp.maximum(top, tile)
        top = jnp.max(top, axis=1, keepdims=True)
        for c, tile in enumerate(tiles):
            emission[8 * j : 8 * j + 8, 128 * c : 128 * c + 128] = jnp.exp(tile - top)


def chain_kernel(
    emission, place, own_scores, pair_scores, own_t, other_t, own_turned, other_turned,
    out, chain, done, part, gain, sums, gains, ordered,
):
    core = lax.axis_index("state")
    half, states = own_t.shape
    rows = place.shape[0]
    frames = rows // 8
    own_rows = rows // 2
    shape = (rows, 128)

    def advance(x):
        last = x[rows - 8 : rows]
        return jnp.concatenate([last[4:8], last[0:4], x[0 : rows - 8]], axis=0)

    def settle(k):
        total = jnp.broadcast_to(jnp.sum(part[...], axis=1, keepdims=True) * gain[...], shape)
        sums[...] = jnp.where(place[...] == k - 1.0, total, sums[...])
        return total

    def spread(k, predicted, scale, index, first=False):
        mask = place[...] == k
        sum_tile = None
        for c in range(states // 128):
            at = slice(128 * c, 128 * c + 128)
            ahead = predicted[:, at]
            weighted = ahead * emission[:, at]
            sum_tile = weighted if sum_tile is None else sum_tile + weighted
            result = weighted if index == 0 else ahead
            done[:, at] = result if first else jnp.where(mask, result, done[:, at])
            chain[:, at] = advance(weighted * scale).astype(bf16)
        part[...] = sum_tile

    def run(index):
        if index == 0:
            line = slice(own_rows, own_rows + 1)
            first = jnp.concatenate(
                [p[c, line, :] for p in (own_scores, pair_scores) for c in range(half // 128)], axis=1
            )
            first = first / jnp.sum(first, axis=1, keepdims=True)
        else:
            first = jnp.full((1, states), 1.0 / states, f32)
        gain[...] = jnp.full(shape, SCALE, f32)
        gains[...] = jnp.full(shape, SCALE, f32)
        sums[...] = jnp.full(shape, SCALE, f32)
        spread(0.0, jnp.broadcast_to(first, (rows, states)), SCALE, index, True)

        def step(k, carry):
            k = k.astype(f32)
            total = settle(k)
            scale = SCALE / advance(total)
            gain[...] = scale
            gains[...] = jnp.where(place[...] == k, scale, gains[...])
            mine, theirs = chain[:, 0:half], chain[:, half:states]
            if index == 0:
                blocks = (own_t[:, 0:half], other_t[:, 0:half], own_t[:, half:], other_t[:, half:])
            else:
                mine_t, other = own_turned, other_turned
                blocks = (mine_t[:, 0:half], mine_t[:, half:], other[:, 0:half], other[:, half:])
            predicted = jnp.concatenate(
                [
                    jnp.dot(mine, blocks[2 * n], preferred_element_type=f32)
                    + jnp.dot(theirs, blocks[2 * n + 1], preferred_element_type=f32)
                    for n in range(2)
                ],
                axis=1,
            )
            spread(k, predicted, scale, index)
            return carry

        lax.fori_loop(1, MAXLEN, step, 0, unroll=UNROLL)
        settle(float(MAXLEN))
        norm = sums[...]
        scale = gains[...] / norm if index == 0 else gains[...] * (1.0 / SCALE)
        logs = jnp.log(norm * (1.0 / SCALE))
        last = states // 128
        for j in range(frames):
            at = j if index == 0 else frames - 1 - j
            own = slice(8 * j + 4, 8 * j + 8)
            for c in range(last):
                cols = slice(128 * c, 128 * c + 128)
                ordered[c, pl.ds(at, 4, stride=frames), :] = done[own, cols] * scale[own]
            ordered[last, pl.ds(at, 4, stride=frames), :] = logs[own]
        for c in range(last):
            out[:, 128 * c : 128 * c + 128] = ordered[c].astype(bf16)
        logs_hi, logs_lo = split_pair(ordered[last])
        out[:, states : states + 128] = logs_hi
        out[:, states + 128 : states + 256] = logs_lo

    for index in range(2):

        @pl.when(core == index)
        def _():
            run(index)


def combine_kernel(own, other, posterior, evidence):
    core = lax.axis_index("state")
    streams, frames, half = posterior.shape
    states = 2 * half
    mine = own[:, 0:half].astype(f32) * other[:, half:states].astype(f32)
    theirs = own[:, half:states].astype(f32) * other[:, 0:half].astype(f32)
    inverse = 1.0 / jnp.sum(mine + theirs, axis=1, keepdims=True)
    posterior[...] = (mine * inverse).astype(bf16).reshape(streams, frames, half)

    def pair(ref):
        return ref[:, states : states + 128].astype(f32) + ref[
            :, states + 128 : states + 256
        ].astype(f32)

    logs = jnp.where(core == 0, pair(own), pair(other))
    shape = (streams * frames, 128)
    row = lax.broadcasted_iota(jnp.int32, shape, 0)
    lane = lax.broadcasted_iota(jnp.int32, shape, 1)
    kept = jnp.where(row % frames == lane + core * (frames // 2), logs, 0.0)
    for b in range(streams):
        line = jnp.sum(kept[b * frames : (b + 1) * frames], axis=0, keepdims=True)
        evidence[b : b + 1, :] = line[:, 0 : frames // 2]


def kernel(body, outs, scratch, vmem, cost, *args, hbm=()):
    in_vmem = pl.BlockSpec(memory_space=VMEM)
    in_hbm = pl.BlockSpec(memory_space=pltpu.HBM)
    args = [
        pltpu.with_memory_space_constraint(a, pltpu.HBM) if n in hbm else a
        for n, a in enumerate(args)
    ]
    return pl.pallas_call(
        body,
        out_shape=[jax.ShapeDtypeStruct(*o) for o in outs],
        in_specs=[in_hbm if n in hbm else in_vmem for n in range(len(args))],
        out_specs=[in_vmem] * len(outs),
        scratch_shapes=scratch,
        compiler_params=pltpu.CompilerParams(vmem_limit_bytes=vmem * MIB),
        cost_estimate=pl.CostEstimate(flops=cost, bytes_accessed=1 * MIB, transcendentals=0),
    )(*args)


def per_device(features, gauss_means, precisions, transitions, initial, reset_flags):
    streams, frames, width = features.shape
    half = gauss_means.shape[0]
    states = transitions.shape[1]
    rows = streams * frames
    blocks = lax.axis_size("tm")
    partner = [(0, 1), (1, 0)]

    pack, scored, w, offsets = kernel(
        front_kernel,
        [
            ((rows, 2 * width + half + 128), bf16),
            ((half // 128, rows + 8, 128), f32),
            ((2 * width, 2 * half), bf16),
            ((8, half), f32),
        ],
        [
            VMEM((rows, 128), f32),
            VMEM((rows, width), f32),
            VMEM((half, width), f32),
            VMEM((half, width), f32),
            VMEM((streams, frames), jnp.int32),
            VMEM((half,), bf16),
            pltpu.SemaphoreType.DMA((2 * PARTS + 3,)),
        ],
        16, 10**9,
        features.reshape(rows, width), gauss_means, precisions, reset_flags, initial,
        hbm=range(5),
    )
    pairs = [(2 * i - 1, 2 * i) for i in range(1, blocks)]
    halo = lax.ppermute(pack, ("tm", "state"), pairs + [(b, a) for a, b in pairs])
    other_t = lax.ppermute(transitions, "state", partner)
    pair = lax.ppermute(scored, "state", partner)
    block = [((half, states), bf16)]
    (own_turned,) = kernel(turn_kernel, block, [], 16, 10**9, transitions)
    (other_turned,) = kernel(turn_kernel, block, [], 16, 10**9, other_t)
    halo_scores, far_scores, place = kernel(
        halo_kernel,
        [((half // 128, rows, 128), f32)] * 2 + [((2 * rows, 128), f32)],
        [], 16, 10**9,
        pack, halo, w, offsets,
    )
    (emission,) = kernel(
        emission_kernel, [((2 * rows, states), f32)], [], 16, 10**9,
        scored, far_scores, pair, halo_scores,
    )
    wide, narrow = VMEM((2 * rows, states), f32), VMEM((2 * rows, 128), f32)
    (out,) = kernel(
        chain_kernel,
        [((rows, states + 256), bf16)],
        [
            VMEM((2 * rows, states), bf16),
            wide, narrow, narrow, narrow, narrow,
            VMEM((states // 128 + 1, rows, 128), f32),
        ],
        24, 10**10,
        emission, place, scored, pair, transitions, other_t, own_turned, other_turned,
    )
    out_other = lax.ppermute(out, "state", partner)
    posterior, evidence = kernel(
        combine_kernel,
        [((streams, frames, half), bf16), ((streams, frames // 2), f32)],
        [], 8, 10**6,
        out, out_other,
    )
    return posterior, evidence


def solution(mesh):
    return jax.shard_map(
        per_device,
        mesh=mesh,
        in_specs=(
            P(None, "tm", None),
            P("state", None),
            P("state", None),
            P("state", None),
            P("state"),
            P(None, "tm"),
        ),
        out_specs=(P(None, "tm", "state"), P(None, ("tm", "state"))),
        check_vma=False,
    )
```
